32 devices in a mesh: ex: 8 (over z, y), par: 4 (over x, core).
Axes of the slice: x: 2, y: 2, z: 4, core: 2. Of those that a mesh axis runs over, the one named last changes fastest.
Arguments:
- gradients: bfloat16 [512, 16384], P('ex', 'par'), may hold values from -6 to 6
- inverse_gram: bfloat16 [16384, 16384], P('par', 'ex'), may hold values from -1 to 3
- hash_words: int32 [4], replicated, may hold values from 1 to 2147483646
Outputs:
- scores: float32 [512, 512], P('par', 'ex')
The draws below stay inside these ranges and needn't reach their ends.
All inputs are finite; a program needn't handle non-finite values.
Results may differ from the reference program's by a relative error of at most 0.0003.
Values may be sent and summed in bfloat16 or wider, within the bound.
A program may use at most 64 MiB of HBM per device.

```python
import math
import jax
import jax.numpy as jnp
from jax import lax

FEATURES = 16384
EXAMPLES = 512
PARAMS = 16384


def draw_inverse_gram(key, part):
    off_key, diag_key = jax.random.split(jax.random.fold_in(key, 11))
    spread = 0.5 / math.sqrt(FEATURES)
    off_part = jax.random.truncated_normal(off_key, -4.0, 4.0, (FEATURES, FEATURES), jnp.float32) * spread
    diagonal = jax.random.uniform(diag_key, (FEATURES,), jnp.float32, 0.5, 2.0)
    diag_ids = jnp.arange(FEATURES)
    return off_part.at[diag_ids, diag_ids].add(diagonal).astype(jnp.bfloat16)


def touch_ends(array, key, smallest, high):
    index_at = [jax.random.randint(jax.random.fold_in(key, axis), (), 0, length) for axis, length in enumerate(array.shape)]
    longest = array.shape.index(max(array.shape))
    next_to = index_at[:longest] + [(index_at[longest] + 1) % array.shape[longest]] + index_at[longest + 1:]
    return array.at[tuple(index_at)].set(smallest).at[tuple(next_to)].set(high)


def shard_levels(own_key, shape, pieces, low, largest):
    loudness = 1.0
    for dim, parts in pieces:
        draws = jax.random.uniform(jax.random.fold_in(jax.random.fold_in(own_key, 6), dim), (parts,), jnp.float32, low / len(pieces), largest / len(pieces))
        loudness = loudness * jnp.repeat(jnp.exp(draws), shape[dim] // parts).reshape((-1,) + (1,) * (len(shape) - 1 - dim))
    return loudness


def scatter_about(own_key, shape, deviation, most, cuts=(), held_as=jnp.bfloat16):
    entries = deviation * jax.random.normal(own_key, shape, jnp.float32)
    if cuts:
        entries = entries * shard_levels(own_key, shape, cuts, -0.22, 0.18)
    return jnp.clip(entries, -most, most).astype(held_as)


def setup_inputs(seed: int = 0) -> dict:
    key_list = jax.random.split(jax.random.key(seed), 4)
    gradients = scatter_about(key_list[0], (EXAMPLES, PARAMS), 1.0, 6.0, ((0, 8), (1, 4)))
    inverse_gram = draw_inverse_gram(jax.random.fold_in(key_list[3], 71), 0)
    hash_words = touch_ends(jax.random.randint(key_list[2], (4,), 1, 2147483647), jax.random.fold_in(key_list[2], 1), 1, 2147483646).astype(jnp.int32)
    return {"gradients": gradients, "inverse_gram": inverse_gram, "hash_words": hash_words}


def shifted(values, amount):
    return lax.shift_right_logical(values, jnp.full(values.shape, amount, jnp.int32))


def hash_table(hash_words, row_start, row_count, col_start, col_count):
    row_ids = lax.broadcasted_iota(jnp.int32, (row_count, col_count), 0) + row_start
    col_ids = lax.broadcasted_iota(jnp.int32, (row_count, col_count), 1) + col_start
    mixed = row_ids * FEATURES + col_ids
    mixed = mixed * (hash_words[0] | 1) + hash_words[1]
    mixed = mixed ^ shifted(mixed, 15)
    mixed = mixed * (hash_words[2] | 1)
    mixed = mixed ^ shifted(mixed, 13)
    mixed = mixed * (hash_words[3] | 1)
    mixed = mixed ^ shifted(mixed, 16)
    top_bit = shifted(mixed, 31)
    return ((1 - 2 * top_bit).astype(jnp.float32) * (FEATURES ** -0.5)).astype(jnp.bfloat16)


def reference(gradients, inverse_gram, hash_words):
    param_count = gradients.shape[1]
    col_width = min(1024, FEATURES)
    block_count = FEATURES // col_width

    def column_block(col_start):
        sign_table = hash_table(hash_words, 0, param_count, col_start, col_width)
        return jnp.dot(gradients, sign_table, preferred_element_type=jnp.float32)

    col_starts = jnp.arange(block_count, dtype=jnp.int32) * col_width
    blocks = lax.map(column_block, col_starts)
    features = jnp.transpose(blocks, (1, 0, 2)).reshape(gradients.shape[0], FEATURES).astype(jnp.bfloat16)
    conditioned = jnp.dot(features, inverse_gram, preferred_element_type=jnp.float32).astype(jnp.bfloat16)
    pairs = jnp.dot(conditioned, features.T, preferred_element_type=jnp.float32)
    return pairs * (FEATURES ** -0.5)
```

```python
import functools

import jax
import jax.numpy as jnp
from jax import lax
from jax.experimental import pallas as pl
from jax.experimental.pallas import tpu as pltpu
from jax.sharding import PartitionSpec as P

FEATURES = 16384


def shifted(values, amount):
    return lax.shift_right_logical(values, jnp.full(values.shape, amount, jnp.int32))


def hash_kernel(tile, words_ref, start_ref, cols_ref, grads_ref, out_ref):
    step = pl.program_id(0)
    depth = grads_ref.shape[1]
    m0 = words_ref[0] | 1
    m2 = words_ref[2] | 1
    m3 = words_ref[3] | 1
    row_base = (start_ref[0] + step * depth) * FEATURES * m0 + words_ref[1]
    rows = lax.broadcasted_iota(jnp.int32, (depth, tile), 0) * (m0 * FEATURES)
    grads = grads_ref[...]
    for spot in range(out_ref.shape[0]):
        first = spot * tile
        mixed = rows + (cols_ref[:, first:first + tile] * m0 + row_base)
        mixed = (mixed ^ shifted(mixed, 15)) * m2
        mixed = (mixed ^ shifted(mixed, 13)) * m3
        signs = jnp.where(mixed < 0, -1.0, 1.0).astype(jnp.bfloat16)
        part = jnp.dot(grads, signs, preferred_element_type=jnp.float32)

        @pl.when(step == 0)
        def _():
            out_ref[spot] = part

        @pl.when(step > 0)
        def _():
            out_ref[spot] += part


def project(words, start, cols, grads, tile):
    rows, amount = grads.shape
    width = cols.shape[1]
    depth = min(512, amount)
    return pl.pallas_call(
        functools.partial(hash_kernel, tile),
        grid=(amount // depth,),
        in_specs=[
            pl.BlockSpec(memory_space=pltpu.SMEM),
            pl.BlockSpec(memory_space=pltpu.SMEM),
            pl.BlockSpec((1, width), lambda k: (0, 0)),
            pl.BlockSpec((rows, depth), lambda k: (0, k)),
        ],
        out_specs=pl.BlockSpec((width // tile, rows, tile), lambda k: (0, 0, 0)),
        out_shape=jax.ShapeDtypeStruct((width // tile, rows, tile), jnp.float32),
        compiler_params=pltpu.CompilerParams(
            dimension_semantics=("arbitrary",), vmem_limit_bytes=48 << 20
        ),
    )(words, start, cols, grads)


MESH = pl.DeviceIdType.MESH


def gather_kernel(ex_n, own_ref, out_ref, keep_sem, up_sem, down_sem, side_sem, recv_sem):
    e = lax.axis_index("ex")
    line, side = e // 2, e % 2
    last = ex_n // 2 - 1
    above, below, beside = lax.rem(e + 2, ex_n), lax.rem(e + ex_n - 2, ex_n), line * 2 + 1 - side
    barrier = pltpu.get_barrier_semaphore()

    def greet(peer):
        pl.semaphore_signal(barrier, inc=1, device_id={"ex": peer}, device_id_type=MESH)

    greet(beside)
    pl.when(line < last)(lambda: greet(above))
    pl.when(line > 0)(lambda: greet(below))
    inside = (line > 0) & (line < last)
    pl.when(inside)(lambda: pl.semaphore_wait(barrier, 3))
    pl.when(jnp.logical_not(inside))(lambda: pl.semaphore_wait(barrier, 2))

    def copy(src, slot, sems, peer):
        return pltpu.make_async_remote_copy(
            src_ref=src,
            dst_ref=out_ref.at[slot],
            send_sem=sems.at[slot],
            recv_sem=recv_sem.at[slot],
            device_id={"ex": peer},
            device_id_type=MESH,
        )

    keep = pltpu.make_async_copy(own_ref, out_ref.at[e], keep_sem)
    keep.start()
    pl.when(line < last)(lambda: copy(own_ref, e, up_sem, above).start())
    pl.when(line > 0)(lambda: copy(own_ref, e, down_sem, below).start())
    copy(own_ref, e, side_sem, beside).start()
    for far in range(1, last + 1):
        low, high = e - 2 * far, e + 2 * far

        @pl.when(line >= far)
        def _():
            copy(out_ref.at[low], low, up_sem, above).wait_recv()
            pl.when(line < last)(lambda: copy(out_ref.at[low], low, up_sem, above).start())
            copy(out_ref.at[low], low, side_sem, beside).start()

        @pl.when(line + far <= last)
        def _():
            copy(out_ref.at[high], high, down_sem, below).wait_recv()
            pl.when(line > 0)(lambda: copy(out_ref.at[high], high, down_sem, below).start())
            copy(out_ref.at[high], high, side_sem, beside).start()

    for spot in range(last + 1):
        mine, other = 2 * spot + side, 2 * spot + 1 - side
        copy(out_ref.at[other], other, side_sem, beside).wait_recv()
        copy(out_ref.at[mine], mine, side_sem, beside).wait_send()

        @pl.when((line < last) & (line >= spot))
        def _():
            copy(out_ref.at[mine], mine, up_sem, above).wait_send()

        @pl.when((line > 0) & (line <= spot))
        def _():
            copy(out_ref.at[mine], mine, down_sem, below).wait_send()

    keep.wait()


def gather(ex_n, own, collective_id):
    return pl.pallas_call(
        functools.partial(gather_kernel, ex_n),
        in_specs=[pl.BlockSpec(memory_space=pltpu.VMEM)],
        out_specs=pl.BlockSpec(memory_space=pl.ANY),
        out_shape=jax.ShapeDtypeStruct((ex_n,) + own.shape, own.dtype),
        scratch_shapes=[pltpu.SemaphoreType.DMA]
        + [pltpu.SemaphoreType.DMA((ex_n,)) for _ in range(4)],
        compiler_params=pltpu.CompilerParams(
            collective_id=collective_id, has_side_effects=True, vmem_limit_bytes=8 << 20
        ),
    )(own)


def scatter_kernel(ex_n, scale, in_ref, out_ref, landed, send_sem, recv_sem):
    e = lax.axis_index("ex")
    rows = out_ref.shape[0]
    barrier = pltpu.get_barrier_semaphore()
    for far in range(1, ex_n):
        peer = lax.rem(e + far, ex_n)
        pl.semaphore_signal(barrier, inc=1, device_id={"ex": peer}, device_id_type=MESH)
    pl.semaphore_wait(barrier, ex_n - 1)
    copies = []
    for far in range(1, ex_n):
        peer = lax.rem(e + far, ex_n)
        copies.append(
            pltpu.make_async_remote_copy(
                src_ref=in_ref.at[pl.ds(pl.multiple_of(peer * rows, rows), rows)],
                dst_ref=landed.at[far],
                send_sem=send_sem.at[far],
                recv_sem=recv_sem.at[far],
                device_id={"ex": peer},
                device_id_type=MESH,
            )
        )
        copies[-1].start()
    total = in_ref[pl.ds(pl.multiple_of(e * rows, rows), rows), :]
    for far in range(1, ex_n):
        copies[far - 1].wait_recv()
        total += landed[far]
    out_ref[...] = total * scale
    for each in copies:
        each.wait_send()


def scatter(ex_n, scale, stacked, collective_id):
    rows, columns = stacked.shape[0] // ex_n, stacked.shape[1]
    return pl.pallas_call(
        functools.partial(scatter_kernel, ex_n, scale),
        in_specs=[pl.BlockSpec(memory_space=pltpu.VMEM)],
        out_specs=pl.BlockSpec(memory_space=pltpu.VMEM),
        out_shape=jax.ShapeDtypeStruct((rows, columns), jnp.float32),
        scratch_shapes=[
            pltpu.VMEM((ex_n, rows, columns), jnp.float32),
            pltpu.SemaphoreType.DMA((ex_n,)),
            pltpu.SemaphoreType.DMA((ex_n,)),
        ],
        compiler_params=pltpu.CompilerParams(
            collective_id=collective_id, has_side_effects=True, vmem_limit_bytes=16 << 20
        ),
    )(stacked)


def fold_kernel(chips, cuts, scale, in_ref, out_ref, near, staged, landed, near_send, near_recv, far_send, far_recv):
    p = lax.axis_index("par")
    x, core = p // 2, p % 2
    rows = in_ref.shape[1] // cuts
    partner = x * 2 + 1 - core
    barrier = pltpu.get_barrier_semaphore()
    pl.semaphore_signal(barrier, inc=1, device_id={"par": partner}, device_id_type=MESH)
    for d in range(1, chips):
        peer = lax.rem(x + d, chips) * 2 + core
        pl.semaphore_signal(barrier, inc=1, device_id={"par": peer}, device_id_type=MESH)
    pl.semaphore_wait(barrier, chips)
    order = [(d, c) for d in list(range(1, chips)) + [0] for c in range(cuts)]
    across, onward = {}, {}
    for d, c in order:
        part = pl.ds(c * rows, rows)
        across[d, c] = pltpu.make_async_remote_copy(
            src_ref=in_ref.at[lax.rem(x + d, chips) * 2 + 1 - core, part],
            dst_ref=near.at[d, part],
            send_sem=near_send.at[d, c],
            recv_sem=near_recv.at[d, c],
            device_id={"par": partner},
            device_id_type=MESH,
        )
        across[d, c].start()
    for d, c in order:
        part = pl.ds(c * rows, rows)
        across[d, c].wait_recv()
        total = in_ref[lax.rem(x + d, chips) * 2 + core, part, :] + near[d, part, :]
        staged[d, part, :] = total
        if d > 0:
            onward[d, c] = pltpu.make_async_remote_copy(
                src_ref=staged.at[d, part],
                dst_ref=landed.at[d, part],
                send_sem=far_send.at[d, c],
                recv_sem=far_recv.at[d, c],
                device_id={"par": lax.rem(x + d, chips) * 2 + core},
                device_id_type=MESH,
            )
            onward[d, c].start()
    for c in range(cuts):
        part = pl.ds(c * rows, rows)
        total = staged[0, part, :]
        for d in range(1, chips):
            onward[d, c].wait_recv()
            total += landed[d, part, :]
        out_ref[part, :] = (total * scale).astype(out_ref.dtype)
    for each in list(across.values()) + list(onward.values()):
        each.wait_send()


def fold(scale, stacked, dtype, collective_id):
    par_n, rows, columns = stacked.shape
    chips = par_n // 2
    cuts = 8 if rows * columns >= 1 << 18 else 2
    hold = pltpu.VMEM((chips, rows, columns), jnp.float32)
    return pl.pallas_call(
        functools.partial(fold_kernel, chips, cuts, scale),
        in_specs=[pl.BlockSpec(memory_space=pltpu.VMEM)],
        out_specs=pl.BlockSpec(memory_space=pltpu.VMEM),
        out_shape=jax.ShapeDtypeStruct((rows, columns), dtype),
        scratch_shapes=[hold, hold, hold]
        + [pltpu.SemaphoreType.DMA((chips, cuts)) for _ in range(4)],
        compiler_params=pltpu.CompilerParams(
            collective_id=collective_id, has_side_effects=True, vmem_limit_bytes=48 << 20
        ),
    )(stacked)


def tiles_kernel(feat_ref, gram_ref, out_ref):
    step = pl.program_id(0)
    tile = out_ref.shape[2]
    for spot in range(out_ref.shape[0]):
        gram = gram_ref[:, spot * tile:(spot + 1) * tile]
        part = jnp.dot(feat_ref[0], gram, preferred_element_type=jnp.float32)

        @pl.when(step == 0)
        def _():
            out_ref[spot] = part

        @pl.when(step > 0)
        def _():
            out_ref[spot] += part


def precondition(blocks, gram, tile):
    count, rows, piece = blocks.shape
    width = gram.shape[1]
    return pl.pallas_call(
        tiles_kernel,
        grid=(count,),
        in_specs=[
            pl.BlockSpec((1, rows, piece), lambda k: (k, 0, 0)),
            pl.BlockSpec((piece, width), lambda k: (k, 0)),
        ],
        out_specs=pl.BlockSpec((width // tile, rows, tile), lambda k: (0, 0, 0)),
        out_shape=jax.ShapeDtypeStruct((width // tile, rows, tile), jnp.float32),
        compiler_params=pltpu.CompilerParams(
            dimension_semantics=("arbitrary",), vmem_limit_bytes=48 << 20
        ),
        cost_estimate=pl.CostEstimate(
            flops=2 * count * rows * piece * width,
            bytes_accessed=2 * count * piece * (rows + width) + 4 * rows * width,
            transcendentals=0,
        ),
    )(blocks, gram)


def rider(src, dst, send_sem, recv_sem, device_id):
    return pltpu.make_async_remote_copy(
        src_ref=src, dst_ref=dst, send_sem=send_sem, recv_sem=recv_sem,
        device_id=device_id, device_id_type=MESH,
    )


ORDER = ((1, 1), (1, 0), (0, 1), (0, 0))


def whole_kernel(
    ex_n, features, tile, early, depth, words_ref, grads_ref, gram_ref, out_ref,
    g2, signs, acc, psend, pown, precv, feats, gram, total, near, staged, far, mine,
    d1_send, d1_recv, d2_send, d2_recv, summed, landed,
    gram_sem, keep_sem, gy_send, gz_send, gc_send, g_recv, gp_recv, px_send, px_recv,
    up_sem, down_sem, side_sem, f_recv, fe_send, fe_recv, fe_keep,
    cc_send, cc_recv, cx_send, cx_recv, d1_ssem, d1_rsem, d2_ssem, d2_rsem, s_send, s_recv,
):
    e, p = lax.axis_index("ex"), lax.axis_index("par")
    z, y, x, c, h, m = e // 2, e % 2, p // 2, p % 2, e // 4, e % 4
    lines, groups = ex_n // 2, ex_n // 4
    last = lines - 1
    half = g2.shape[3]
    amount = g2.shape[4]
    count = feats.shape[0]
    group_rows = feats.shape[3]
    block = gram.shape[0]
    piece = block // 4
    everyone, width = total.shape[1], total.shape[2]
    scale = features ** -0.5

    def others(own, n):
        return [lax.rem(own + d, n) for d in range(1, n)]

    barrier = pltpu.get_barrier_semaphore()
    for peer in others(e, ex_n):
        pl.semaphore_signal(barrier, inc=1, device_id={"ex": peer}, device_id_type=MESH)
    for peer in others(p, 4):
        pl.semaphore_signal(barrier, inc=1, device_id={"par": peer}, device_id_type=MESH)
    pl.semaphore_wait(barrier, ex_n + 2)

    to_y, to_z = {"ex": e + 1 - 2 * y}, {"ex": e + 2 - 4 * (z % 2)}
    to_core, to_x = {"par": x * 2 + 1 - c}, {"par": (1 - x) * 2 + c}
    to_up, to_down = {"ex": lax.rem(e + 2, ex_n)}, {"ex": lax.rem(e + ex_n - 2, ex_n)}
    my, mz, md = m + 1 - 2 * (m % 2), m + 2 - 4 * (m // 2), 3 - m

    gsends = []

    def gcopy(src, slot, part, sems, k, recv, target):
        copy = rider(src, g2.at[c, slot, part], sems.at[k], recv.at[slot, part], target)
        copy.start()
        gsends.append(copy)

    own = [grads_ref.at[pl.ds(part * half, half)] for part in (0, 1)]
    keeps = [pltpu.make_async_copy(own[part], g2.at[c, m, part], keep_sem.at[part]) for part in (0, 1)]
    gcopy(own[0], m, 0, gy_send, 0, g_recv, to_y)
    gcopy(own[1], m, 1, gz_send, 0, g_recv, to_z)
    gcopy(own[1], m, 1, gy_send, 1, g_recv, to_y)
    gcopy(own[0], m, 0, gz_send, 1, g_recv, to_z)
    for part in (0, 1):
        keeps[part].start()
        gcopy(own[part], m, part, gc_send, part, gp_recv, to_core)
    loads = []
    for k in range(4):
        rows = pl.ds(k * piece, piece)
        loads.append(pltpu.make_async_copy(gram_ref.at[rows], gram.at[rows], gram_sem.at[k]))
        loads[-1].start()

    def arrived(slot, part, recv, core):
        spot = g2.at[core, slot, part]
        rider(spot, spot, gy_send.at[0], recv.at[slot, part], to_y).wait_recv()

    def first_halves():
        arrived(my, 0, g_recv, c)
        gcopy(g2.at[c, my, 0], my, 0, gz_send, 2, g_recv, to_z)
        gcopy(g2.at[c, my, 0], my, 0, gc_send, 2, gp_recv, to_core)
        arrived(mz, 1, g_recv, c)
        gcopy(g2.at[c, mz, 1], mz, 1, gy_send, 2, g_recv, to_y)
        gcopy(g2.at[c, mz, 1], mz, 1, gc_send, 3, gp_recv, to_core)

    def second_halves():
        arrived(my, 1, g_recv, c)
        gcopy(g2.at[c, my, 1], my, 1, gc_send, 4, gp_recv, to_core)
        arrived(mz, 0, g_recv, c)
        gcopy(g2.at[c, mz, 0], mz, 0, gc_send, 5, gp_recv, to_core)

    def last_halves():
        for part in (0, 1):
            arrived(md, part, g_recv, c)
            gcopy(g2.at[c, md, part], md, part, gc_send, 6 + part, gp_recv, to_core)
        for slot in range(4):
            for part in (0, 1):
                arrived(slot, part, gp_recv, 1 - c)
        for keep in keeps:
            keep.wait()

    m0 = words_ref[0] | 1
    m2 = words_ref[2] | 1
    m3 = words_ref[3] | 1
    spots = lax.broadcasted_iota(jnp.int32, (2 * tile, 1), 0)
    jump = jnp.where(spots < tile, ((1 - x) * 2 + c) * block, (x * 2 + c) * block - tile)
    offsets = (spots + jump) * m0
    across = lax.broadcasted_iota(jnp.int32, (1, depth), 1) * (m0 * features)
    steps = amount // depth

    def make_signs(t, core, step):
        first = ((x * 2 + core) * amount + step * depth) * features
        base = (first + m * piece + t * tile) * m0 + words_ref[1]
        mixed = offsets + (across + base)
        mixed = (mixed ^ shifted(mixed, 15)) * m2
        mixed = (mixed ^ shifted(mixed, 13)) * m3
        return jnp.where(mixed < 0, -1.0, 1.0).astype(jnp.bfloat16)

    def columns(step):
        return pl.ds(pl.multiple_of(step * depth, depth), depth)

    def add_in(s, core, step):
        g = g2[core, :, :, :, columns(step)].reshape(group_rows, depth)
        acc[...] += lax.dot_general(
            s, g, (((1,), (1,)), ((), ())), preferred_element_type=jnp.float32
        )

    def prepare(t):
        @pl.loop(0, 2 * steps)
        def _(k):
            signs[t, k] = make_signs(t, k // steps, k % steps)

    prepare(0)
    if early > 1:
        prepare(1)
    first_halves()
    if early > 2:
        prepare(2)
    if early > 3:
        prepare(3)
    second_halves()
    last_halves()

    def slot(t, s):
        return feats.at[t, s % 4, s // 4]

    def send(t, s, sems, target):
        return rider(slot(t, s), slot(t, s), sems.at[t, s], f_recv.at[t, s], target)

    def x_copy(t):
        return rider(psend.at[t], precv.at[t], px_send.at[t], px_recv.at[t], to_x)

    def finish(t):
        x_copy(t).wait_recv()
        done = (pown[t] + precv[t]) * scale
        feats[t, m, h] = done.T.astype(jnp.bfloat16)
        pl.when(z < last)(lambda: send(t, e, up_sem, to_up).start())
        pl.when(z > 0)(lambda: send(t, e, down_sem, to_down).start())
        send(t, e, side_sem, to_y).start()

    def relay(t, hop):
        @pl.when(z >= hop)
        def _():
            low = e - 2 * hop
            send(t, low, up_sem, to_up).wait_recv()
            pl.when(z < last)(lambda: send(t, low, up_sem, to_up).start())
            send(t, low, side_sem, to_y).start()

        @pl.when(z + hop <= last)
        def _():
            high = e + 2 * hop
            send(t, high, down_sem, to_down).wait_recv()
            pl.when(z > 0)(lambda: send(t, high, down_sem, to_down).start())
            send(t, high, side_sem, to_y).start()

    def produced(t):
        psend[t] = acc[:tile]
        pown[t] = acc[tile:]
        x_copy(t).start()

    def service(t):
        pl.when(t >= 1)(lambda: finish(t - 1))
        for hop in range(1, lines):
            pl.when(t >= hop + 1)(lambda: relay(t - hop - 1, hop))

    @pl.loop(0, early)
    def _(t):
        acc[...] = jnp.zeros_like(acc)

        @pl.loop(0, 2 * steps)
        def _(k):
            add_in(signs[t, k], k // steps, k % steps)

        produced(t)
        service(t)

    @pl.loop(early, count)
    def _(t):
        acc[...] = jnp.zeros_like(acc)

        @pl.loop(0, 2 * steps)
        def _(k):
            add_in(make_signs(t, k // steps, k % steps), k // steps, k % steps)

        produced(t)
        service(t)

    for load in loads:
        load.wait()
    holder = e // (ex_n // 4)
    per = width // tile

    def deal(t, q, act):
        spot = (e % 2) * 2 + q // 2
        src = feats.at[t, spot]
        dst = mine.at[t % per]

        @pl.when((p == holder) & (p == q))
        def _():
            act(pltpu.make_async_copy(src, dst, fe_keep.at[t % per]), False)

        @pl.when((p == holder) & (p != q))
        def _():
            act(rider(src, dst, fe_send.at[t, q // 2], fe_recv.at[t % per], {"par": q}), True)

    def go(copy, remote):
        copy.start()

    def sent(copy, remote):
        if remote:
            copy.wait_send()

    def multiply(t):
        for line in range(lines):
            send(t, 2 * line + 1 - y, side_sem, to_y).wait_recv()
        for q in (t // per, 2 + t // per):
            deal(t, q, go)
        lhs = jnp.concatenate([feats[t, k].reshape(everyone, tile) for k in range(4)], axis=1)
        for q in range(4):
            cols = pl.ds(q * width, width)
            rhs = jnp.concatenate(
                [gram[k * piece + t * tile:k * piece + (t + 1) * tile, q * width:(q + 1) * width] for k in range(4)], axis=0
            )
            part = jnp.dot(lhs, rhs, preferred_element_type=jnp.float32)
            if t == 0:
                total[q] = part
            else:
                total[q] += part

    events = []
    finish(count - 1)
    ready = 0
    for t in range(count, count + lines - 1):
        for hop in range(1, lines):
            if t - hop - 1 < count:
                relay(t - hop - 1, hop)
            if hop % 2 == 1 and ready < count - 2:
                multiply(ready)
                ready += 1
    relay(count - 1, last) if lines > 1 else None
    for t in range(ready, count):
        multiply(t)

    rows_of = everyone // 4

    def rows(owner):
        return pl.ds(pl.multiple_of(owner * rows_of, rows_of), rows_of)

    def place(dx, dc, sx, sc):
        return ((sx + dx) % 2) * 2 + (sc + dc) % 2

    def near_copy(qx, owner):
        return rider(
            total.at[qx * 2 + 1 - c, rows(owner)], near.at[qx, rows(owner)],
            cc_send.at[qx, owner], cc_recv.at[qx, owner], to_core,
        )

    def far_copy(owner):
        return rider(
            staged.at[rows(owner)], far.at[rows(owner)], cx_send.at[owner], cx_recv.at[owner], to_x
        )

    for dx, dc in ORDER:
        near_copy(1 - x, place(dx, dc, 1 - x, 1 - c)).start()
    for dx, dc in ORDER:
        near_copy(x, place(dx, dc, x, 1 - c)).start()
    for dx, dc in ORDER:
        owner = place(dx, dc, 1 - x, c)
        near_copy(1 - x, owner).wait_recv()
        staged[rows(owner), :] = total[(1 - x) * 2 + c, rows(owner), :] + near[1 - x, rows(owner), :]
        far_copy(owner).start()

    for k in range(per):
        q_spot = mine.at[k]

        @pl.when(p == holder)
        def _():
            pltpu.make_async_copy(q_spot, q_spot, fe_keep.at[k]).wait()

        @pl.when(p != holder)
        def _():
            rider(q_spot, q_spot, fe_send.at[0, 0], fe_recv.at[k], to_core).wait_recv()

    def d1_copy(k):
        return rider(d1_send.at[k], d1_recv.at[k], d1_ssem.at[k], d1_rsem.at[k], to_core)

    d2_copy = rider(d2_send, d2_recv, d2_ssem, d2_rsem, to_x)
    for dx, dc in ORDER:
        owner = place(dx, dc, x, c)
        near_copy(x, owner).wait_recv()
        half_sum = total[x * 2 + c, rows(owner), :] + near[x, rows(owner), :]
        far_copy(owner).wait_recv()
        done = (half_sum + far[rows(owner), :]).astype(jnp.bfloat16)
        rhs = jnp.concatenate([mine[k].reshape(everyone, tile) for k in range(per)], axis=1)
        part = lax.dot_general(
            rhs, done, (((1,), (1,)), ((), ())), preferred_element_type=jnp.float32
        )
        if dc == 1:
            d1_send[1 - dx] = part
            d1_copy(1 - dx).start()
        elif dx == 1:
            d1_copy(0).wait_recv()
            d2_send[...] = part + d1_recv[0]
            d2_copy.start()
        else:
            d1_copy(1).wait_recv()
            part = part + d1_recv[1]
            d2_copy.wait_recv()
            part = part + d2_recv[...]
            summed[...] = part.reshape(summed.shape)

    def last_copy(k):
        peer = lax.rem(e + k, ex_n)
        return rider(summed.at[peer], landed.at[k], s_send.at[k], s_recv.at[k], {"ex": peer})

    for k in range(1, ex_n):
        last_copy(k).start()
    final = summed[e]
    for k in range(1, ex_n):
        last_copy(k).wait_recv()
        final += landed[k]
    out_ref[...] = (final * scale).T

    for copy in gsends:
        copy.wait_send()
    for t in range(count):
        x_copy(t).wait_send()
        for q in (t // per, 2 + t // per):
            deal(t, q, sent)
        send(t, e, side_sem, to_y).wait_send()
        for line in range(lines):
            s = 2 * line + y
            pl.when(line != z)(lambda: send(t, s, side_sem, to_y).wait_send())
            pl.when((z < last) & (z >= line))(lambda: send(t, s, up_sem, to_up).wait_send())
            pl.when((z > 0) & (z <= line))(lambda: send(t, s, down_sem, to_down).wait_send())
    for owner in range(4):
        near_copy(0, owner).wait_send()
        near_copy(1, owner).wait_send()
        far_copy(owner).wait_send()
    d1_copy(0).wait_send()
    d1_copy(1).wait_send()
    d2_copy.wait_send()
    for k in range(1, ex_n):
        last_copy(k).wait_send()


def fused(ex_n, par_n, gradients, inverse_gram, hash_words):
    rows, amount = gradients.shape
    block, width_e = inverse_gram.shape
    features, everyone = block * par_n, rows * ex_n
    tile, depth = 128, min(2048, amount)
    count, width, groups = block // 4 // tile, width_e // 4, ex_n // 4
    early = min(4, count)
    group = 4 * rows
    owned = everyone // 4
    vmem, dma, f32, bf16 = pltpu.VMEM, pltpu.SemaphoreType.DMA, jnp.float32, jnp.bfloat16
    return pl.pallas_call(
        functools.partial(whole_kernel, ex_n, features, tile, early, depth),
        in_specs=[
            pl.BlockSpec(memory_space=pltpu.SMEM),
            pl.BlockSpec(memory_space=pl.ANY),
            pl.BlockSpec(memory_space=pl.ANY),
        ],
        out_specs=pl.BlockSpec(memory_space=pltpu.VMEM),
        out_shape=jax.ShapeDtypeStruct((owned, rows), f32),
        scratch_shapes=[
            vmem((2, 4, 2, rows // 2, amount), bf16),
            vmem((early, 2 * amount // depth, 2 * tile, depth), bf16),
            vmem((2 * tile, group), f32),
            vmem((count, tile, group), f32),
            vmem((count, tile, group), f32),
            vmem((count, tile, group), f32),
            vmem((count, 4, groups, group, tile), bf16),
            vmem((block, width_e), bf16),
            vmem((4, everyone, width), f32),
            vmem((2, everyone, width), f32),
            vmem((everyone, width), f32),
            vmem((everyone, width), f32),
            vmem((width // tile, groups, group, tile), bf16),
            vmem((2, everyone, owned), f32),
            vmem((2, everyone, owned), f32),
            vmem((everyone, owned), f32),
            vmem((everyone, owned), f32),
            vmem((ex_n, rows, owned), f32),
            vmem((ex_n, rows, owned), f32),
            dma((4,)), dma((2,)), dma((3,)), dma((3,)), dma((8,)), dma((4, 2)), dma((4, 2)),
            dma((count,)), dma((count,)),
            dma((count, ex_n)), dma((count, ex_n)), dma((count, ex_n)), dma((count, ex_n)),
            dma((count, 2)), dma((width // tile,)), dma((width // tile,)),
            dma((2, 4)), dma((2, 4)), dma((4,)), dma((4,)),
            dma((2,)), dma((2,)), dma, dma, dma((ex_n,)), dma((ex_n,)),
        ],
        compiler_params=pltpu.CompilerParams(
            collective_id=7, has_side_effects=True, vmem_limit_bytes=66_000_000
        ),
    )(hash_words, gradients, inverse_gram)


def fits(ex_n, par_n, gradients, inverse_gram):
    rows = gradients.shape[0]
    block, width_e = inverse_gram.shape
    return (
        par_n == 4 and ex_n == 2 * par_n and width_e % 512 == 0 and block % 512 == 0
        and rows % 32 == 0 and rows * ex_n % 512 == 0
    )


def per_device(ex_n, par_n, gradients, inverse_gram, hash_words):
    if fits(ex_n, par_n, gradients, inverse_gram):
        return fused(ex_n, par_n, gradients, inverse_gram, hash_words)
    amount = gradients.shape[1]
    feat_par, feat_ex = inverse_gram.shape
    piece = feat_par // ex_n
    e, p = lax.axis_index("ex"), lax.axis_index("par")
    ids = jnp.arange(feat_ex, dtype=jnp.int32)
    cols = (ids // piece) * feat_par + e * piece + ids % piece
    everyone = gather(ex_n, gradients, 1).reshape(-1, amount)
    partial = project(hash_words, (p * amount)[None], cols[None, :], everyone, piece)
    mine = fold(FEATURES ** (-0.5), partial, jnp.bfloat16, 4)
    blocks = gather(ex_n, mine, 2)
    mine, blocks = lax.optimization_barrier((mine, blocks))
    pairs = []
    for src_e in range(ex_n):
        for src_p in range(par_n):
            pairs.append((src_e * par_n + src_p, src_p * ex_n + src_e))
    moved = lax.ppermute(mine, ("ex", "par"), pairs)
    parts = precondition(blocks, inverse_gram, piece)
    conditioned = fold(1.0, parts, jnp.bfloat16, 5)
    pairs = lax.dot_general(
        conditioned,
        moved,
        (((1,), (1,)), ((), ())),
        preferred_element_type=jnp.float32,
    )
    rows = fold(1.0, pairs.reshape(par_n, -1, pairs.shape[1]), jnp.float32, 6)
    return scatter(ex_n, FEATURES ** (-0.5), rows.T, 3).T


def solution(mesh):
    return jax.shard_map(
        functools.partial(per_device, mesh.shape["ex"], mesh.shape["par"]),
        mesh=mesh,
        in_specs=(P("ex", "par"), P("par", "ex"), P()),
        out_specs=P("par", "ex"),
        check_vma=False,
    )
```

```python
import functools

import jax
import jax.numpy as jnp
from jax import lax
from jax.experimental import pallas as pl
from jax.experimental.pallas import tpu as pltpu
from jax.sharding import PartitionSpec as P

FEATURES = 16384


def shifted(values, amount):
    return lax.shift_right_logical(values, jnp.full(values.shape, amount, jnp.int32))


def hash_kernel(tile, words_ref, start_ref, cols_ref, grads_ref, out_ref):
    step = pl.program_id(0)
    depth = grads_ref.shape[1]
    m0 = words_ref[0] | 1
    m2 = words_ref[2] | 1
    m3 = words_ref[3] | 1
    row_base = (start_ref[0] + step * depth) * FEATURES * m0 + words_ref[1]
    rows = lax.broadcasted_iota(jnp.int32, (depth, tile), 0) * (m0 * FEATURES)
    grads = grads_ref[...]
    for spot in range(out_ref.shape[0]):
        first = spot * tile
        mixed = rows + (cols_ref[:, first:first + tile] * m0 + row_base)
        mixed = (mixed ^ shifted(mixed, 15)) * m2
        mixed = (mixed ^ shifted(mixed, 13)) * m3
        signs = jnp.where(mixed < 0, -1.0, 1.0).astype(jnp.bfloat16)
        part = jnp.dot(grads, signs, preferred_element_type=jnp.float32)

        @pl.when(step == 0)
        def _():
            out_ref[spot] = part

        @pl.when(step > 0)
        def _():
            out_ref[spot] += part


def project(words, start, cols, grads, tile):
    rows, amount = grads.shape
    width = cols.shape[1]
    depth = min(512, amount)
    return pl.pallas_call(
        functools.partial(hash_kernel, tile),
        grid=(amount // depth,),
        in_specs=[
            pl.BlockSpec(memory_space=pltpu.SMEM),
            pl.BlockSpec(memory_space=pltpu.SMEM),
            pl.BlockSpec((1, width), lambda k: (0, 0)),
            pl.BlockSpec((rows, depth), lambda k: (0, k)),
        ],
        out_specs=pl.BlockSpec((width // tile, rows, tile), lambda k: (0, 0, 0)),
        out_shape=jax.ShapeDtypeStruct((width // tile, rows, tile), jnp.float32),
        compiler_params=pltpu.CompilerParams(
            dimension_semantics=("arbitrary",), vmem_limit_bytes=48 << 20
        ),
    )(words, start, cols, grads)


MESH = pl.DeviceIdType.MESH


def gather_kernel(ex_n, own_ref, out_ref, keep_sem, up_sem, down_sem, side_sem, recv_sem):
    e = lax.axis_index("ex")
    line, side = e // 2, e % 2
    last = ex_n // 2 - 1
    above, below, beside = lax.rem(e + 2, ex_n), lax.rem(e + ex_n - 2, ex_n), line * 2 + 1 - side
    barrier = pltpu.get_barrier_semaphore()

    def greet(peer):
        pl.semaphore_signal(barrier, inc=1, device_id={"ex": peer}, device_id_type=MESH)

    greet(beside)
    pl.when(line < last)(lambda: greet(above))
    pl.when(line > 0)(lambda: greet(below))
    inside = (line > 0) & (line < last)
    pl.when(inside)(lambda: pl.semaphore_wait(barrier, 3))
    pl.when(jnp.logical_not(inside))(lambda: pl.semaphore_wait(barrier, 2))

    def copy(src, slot, sems, peer):
        return pltpu.make_async_remote_copy(
            src_ref=src,
            dst_ref=out_ref.at[slot],
            send_sem=sems.at[slot],
            recv_sem=recv_sem.at[slot],
            device_id={"ex": peer},
            device_id_type=MESH,
        )

    keep = pltpu.make_async_copy(own_ref, out_ref.at[e], keep_sem)
    keep.start()
    pl.when(line < last)(lambda: copy(own_ref, e, up_sem, above).start())
    pl.when(line > 0)(lambda: copy(own_ref, e, down_sem, below).start())
    copy(own_ref, e, side_sem, beside).start()
    for far in range(1, last + 1):
        low, high = e - 2 * far, e + 2 * far

        @pl.when(line >= far)
        def _():
            copy(out_ref.at[low], low, up_sem, above).wait_recv()
            pl.when(line < last)(lambda: copy(out_ref.at[low], low, up_sem, above).start())
            copy(out_ref.at[low], low, side_sem, beside).start()

        @pl.when(line + far <= last)
        def _():
            copy(out_ref.at[high], high, down_sem, below).wait_recv()
            pl.when(line > 0)(lambda: copy(out_ref.at[high], high, down_sem, below).start())
            copy(out_ref.at[high], high, side_sem, beside).start()

    for spot in range(last + 1):
        mine, other = 2 * spot + side, 2 * spot + 1 - side
        copy(out_ref.at[other], other, side_sem, beside).wait_recv()
        copy(out_ref.at[mine], mine, side_sem, beside).wait_send()

        @pl.when((line < last) & (line >= spot))
        def _():
            copy(out_ref.at[mine], mine, up_sem, above).wait_send()

        @pl.when((line > 0) & (line <= spot))
        def _():
            copy(out_ref.at[mine], mine, down_sem, below).wait_send()

    keep.wait()


def gather(ex_n, own, collective_id):
    return pl.pallas_call(
        functools.partial(gather_kernel, ex_n),
        in_specs=[pl.BlockSpec(memory_space=pltpu.VMEM)],
        out_specs=pl.BlockSpec(memory_space=pl.ANY),
        out_shape=jax.ShapeDtypeStruct((ex_n,) + own.shape, own.dtype),
        scratch_shapes=[pltpu.SemaphoreType.DMA]
        + [pltpu.SemaphoreType.DMA((ex_n,)) for _ in range(4)],
        compiler_params=pltpu.CompilerParams(
            collective_id=collective_id, has_side_effects=True, vmem_limit_bytes=8 << 20
        ),
    )(own)


def scatter_kernel(ex_n, scale, in_ref, out_ref, landed, send_sem, recv_sem):
    e = lax.axis_index("ex")
    rows = out_ref.shape[0]
    barrier = pltpu.get_barrier_semaphore()
    for far in range(1, ex_n):
        peer = lax.rem(e + far, ex_n)
        pl.semaphore_signal(barrier, inc=1, device_id={"ex": peer}, device_id_type=MESH)
    pl.semaphore_wait(barrier, ex_n - 1)
    copies = []
    for far in range(1, ex_n):
        peer = lax.rem(e + far, ex_n)
        copies.append(
            pltpu.make_async_remote_copy(
                src_ref=in_ref.at[pl.ds(pl.multiple_of(peer * rows, rows), rows)],
                dst_ref=landed.at[far],
                send_sem=send_sem.at[far],
                recv_sem=recv_sem.at[far],
                device_id={"ex": peer},
                device_id_type=MESH,
            )
        )
        copies[-1].start()
    total = in_ref[pl.ds(pl.multiple_of(e * rows, rows), rows), :]
    for far in range(1, ex_n):
        copies[far - 1].wait_recv()
        total += landed[far]
    out_ref[...] = total * scale
    for each in copies:
        each.wait_send()


def scatter(ex_n, scale, stacked, collective_id):
    rows, columns = stacked.shape[0] // ex_n, stacked.shape[1]
    return pl.pallas_call(
        functools.partial(scatter_kernel, ex_n, scale),
        in_specs=[pl.BlockSpec(memory_space=pltpu.VMEM)],
        out_specs=pl.BlockSpec(memory_space=pltpu.VMEM),
        out_shape=jax.ShapeDtypeStruct((rows, columns), jnp.float32),
        scratch_shapes=[
            pltpu.VMEM((ex_n, rows, columns), jnp.float32),
            pltpu.SemaphoreType.DMA((ex_n,)),
            pltpu.SemaphoreType.DMA((ex_n,)),
        ],
        compiler_params=pltpu.CompilerParams(
            collective_id=collective_id, has_side_effects=True, vmem_limit_bytes=16 << 20
        ),
    )(stacked)


def fold_kernel(chips, cuts, scale, in_ref, out_ref, near, staged, landed, near_send, near_recv, far_send, far_recv):
    p = lax.axis_index("par")
    x, core = p // 2, p % 2
    rows = in_ref.shape[1] // cuts
    partner = x * 2 + 1 - core
    barrier = pltpu.get_barrier_semaphore()
    pl.semaphore_signal(barrier, inc=1, device_id={"par": partner}, device_id_type=MESH)
    for d in range(1, chips):
        peer = lax.rem(x + d, chips) * 2 + core
        pl.semaphore_signal(barrier, inc=1, device_id={"par": peer}, device_id_type=MESH)
    pl.semaphore_wait(barrier, chips)
    order = [(d, c) for d in list(range(1, chips)) + [0] for c in range(cuts)]
    across, onward = {}, {}
    for d, c in order:
        part = pl.ds(c * rows, rows)
        across[d, c] = pltpu.make_async_remote_copy(
            src_ref=in_ref.at[lax.rem(x + d, chips) * 2 + 1 - core, part],
            dst_ref=near.at[d, part],
            send_sem=near_send.at[d, c],
            recv_sem=near_recv.at[d, c],
            device_id={"par": partner},
            device_id_type=MESH,
        )
        across[d, c].start()
    for d, c in order:
        part = pl.ds(c * rows, rows)
        across[d, c].wait_recv()
        total = in_ref[lax.rem(x + d, chips) * 2 + core, part, :] + near[d, part, :]
        staged[d, part, :] = total
        if d > 0:
            onward[d, c] = pltpu.make_async_remote_copy(
                src_ref=staged.at[d, part],
                dst_ref=landed.at[d, part],
                send_sem=far_send.at[d, c],
                recv_sem=far_recv.at[d, c],
                device_id={"par": lax.rem(x + d, chips) * 2 + core},
                device_id_type=MESH,
            )
            onward[d, c].start()
    for c in range(cuts):
        part = pl.ds(c * rows, rows)
        total = staged[0, part, :]
        for d in range(1, chips):
            onward[d, c].wait_recv()
            total += landed[d, part, :]
        out_ref[part, :] = (total * scale).astype(out_ref.dtype)
    for each in list(across.values()) + list(onward.values()):
        each.wait_send()


def fold(scale, stacked, dtype, collective_id):
    par_n, rows, columns = stacked.shape
    chips = par_n // 2
    cuts = 8 if rows * columns >= 1 << 18 else 2
    hold = pltpu.VMEM((chips, rows, columns), jnp.float32)
    return pl.pallas_call(
        functools.partial(fold_kernel, chips, cuts, scale),
        in_specs=[pl.BlockSpec(memory_space=pltpu.VMEM)],
        out_specs=pl.BlockSpec(memory_space=pltpu.VMEM),
        out_shape=jax.ShapeDtypeStruct((rows, columns), dtype),
        scratch_shapes=[hold, hold, hold]
        + [pltpu.SemaphoreType.DMA((chips, cuts)) for _ in range(4)],
        compiler_params=pltpu.CompilerParams(
            collective_id=collective_id, has_side_effects=True, vmem_limit_bytes=48 << 20
        ),
    )(stacked)


def tiles_kernel(feat_ref, gram_ref, out_ref):
    step = pl.program_id(0)
    tile = out_ref.shape[2]
    for spot in range(out_ref.shape[0]):
        gram = gram_ref[:, spot * tile:(spot + 1) * tile]
        part = jnp.dot(feat_ref[0], gram, preferred_element_type=jnp.float32)

        @pl.when(step == 0)
        def _():
            out_ref[spot] = part

        @pl.when(step > 0)
        def _():
            out_ref[spot] += part


def precondition(blocks, gram, tile):
    count, rows, piece = blocks.shape
    width = gram.shape[1]
    return pl.pallas_call(
        tiles_kernel,
        grid=(count,),
        in_specs=[
            pl.BlockSpec((1, rows, piece), lambda k: (k, 0, 0)),
            pl.BlockSpec((piece, width), lambda k: (k, 0)),
        ],
        out_specs=pl.BlockSpec((width // tile, rows, tile), lambda k: (0, 0, 0)),
        out_shape=jax.ShapeDtypeStruct((width // tile, rows, tile), jnp.float32),
        compiler_params=pltpu.CompilerParams(
            dimension_semantics=("arbitrary",), vmem_limit_bytes=48 << 20
        ),
        cost_estimate=pl.CostEstimate(
            flops=2 * count * rows * piece * width,
            bytes_accessed=2 * count * piece * (rows + width) + 4 * rows * width,
            transcendentals=0,
        ),
    )(blocks, gram)


def rider(src, dst, send_sem, recv_sem, device_id):
    return pltpu.make_async_remote_copy(
        src_ref=src, dst_ref=dst, send_sem=send_sem, recv_sem=recv_sem,
        device_id=device_id, device_id_type=MESH,
    )


def whole_kernel(
    ex_n, features, tile, early, depth, words_ref, grads_ref, gram_ref, out_ref,
    g2, signs, acc, psend, pown, precv, feats, gram, total, near, staged, far, marks, far_marks,
    mine, pairs, landed,
    gram_sem, keep_sem, gy_send, gz_send, gc_send, g_recv, gp_recv, px_send, px_recv,
    up_sem, down_sem, side_sem, f_recv, fe_send, fe_recv, fe_keep,
    cc_send, cc_recv, cx_send, cx_recv, cm_send, cm_recv, s_send, s_recv,
):
    e, p = lax.axis_index("ex"), lax.axis_index("par")
    z, y, x, c, h, m = e // 2, e % 2, p // 2, p % 2, e // 4, e % 4
    lines, groups = ex_n // 2, ex_n // 4
    last = lines - 1
    half = g2.shape[3]
    amount = g2.shape[4]
    count = feats.shape[0]
    group_rows = feats.shape[3]
    block = gram.shape[0]
    piece = block // 4
    everyone, width = total.shape[1], total.shape[2]
    scale = features ** -0.5

    def others(own, n):
        return [lax.rem(own + d, n) for d in range(1, n)]

    barrier = pltpu.get_barrier_semaphore()
    for peer in others(e, ex_n):
        pl.semaphore_signal(barrier, inc=1, device_id={"ex": peer}, device_id_type=MESH)
    for peer in others(p, 4):
        pl.semaphore_signal(barrier, inc=1, device_id={"par": peer}, device_id_type=MESH)
    pl.semaphore_wait(barrier, ex_n + 2)

    to_y, to_z = {"ex": e + 1 - 2 * y}, {"ex": e + 2 - 4 * (z % 2)}
    to_core, to_x = {"par": x * 2 + 1 - c}, {"par": (1 - x) * 2 + c}
    to_up, to_down = {"ex": lax.rem(e + 2, ex_n)}, {"ex": lax.rem(e + ex_n - 2, ex_n)}
    my, mz, md = m + 1 - 2 * (m % 2), m + 2 - 4 * (m // 2), 3 - m

    gsends = []

    def gcopy(src, slot, part, sems, k, recv, target):
        copy = rider(src, g2.at[c, slot, part], sems.at[k], recv.at[slot, part], target)
        copy.start()
        gsends.append(copy)

    own = [grads_ref.at[pl.ds(part * half, half)] for part in (0, 1)]
    keeps = [pltpu.make_async_copy(own[part], g2.at[c, m, part], keep_sem.at[part]) for part in (0, 1)]
    gcopy(own[0], m, 0, gy_send, 0, g_recv, to_y)
    gcopy(own[1], m, 1, gz_send, 0, g_recv, to_z)
    gcopy(own[1], m, 1, gy_send, 1, g_recv, to_y)
    gcopy(own[0], m, 0, gz_send, 1, g_recv, to_z)
    for part in (0, 1):
        keeps[part].start()
        gcopy(own[part], m, part, gc_send, part, gp_recv, to_core)
    loads = []
    for k in range(4):
        rows = pl.ds(k * piece, piece)
        loads.append(pltpu.make_async_copy(gram_ref.at[rows], gram.at[rows], gram_sem.at[k]))
        loads[-1].start()

    def arrived(slot, part, recv, core):
        spot = g2.at[core, slot, part]
        rider(spot, spot, gy_send.at[0], recv.at[slot, part], to_y).wait_recv()

    def first_halves():
        arrived(my, 0, g_recv, c)
        gcopy(g2.at[c, my, 0], my, 0, gz_send, 2, g_recv, to_z)
        gcopy(g2.at[c, my, 0], my, 0, gc_send, 2, gp_recv, to_core)
        arrived(mz, 1, g_recv, c)
        gcopy(g2.at[c, mz, 1], mz, 1, gy_send, 2, g_recv, to_y)
        gcopy(g2.at[c, mz, 1], mz, 1, gc_send, 3, gp_recv, to_core)

    def second_halves():
        arrived(my, 1, g_recv, c)
        gcopy(g2.at[c, my, 1], my, 1, gc_send, 4, gp_recv, to_core)
        arrived(mz, 0, g_recv, c)
        gcopy(g2.at[c, mz, 0], mz, 0, gc_send, 5, gp_recv, to_core)

    def last_halves():
        for part in (0, 1):
            arrived(md, part, g_recv, c)
            gcopy(g2.at[c, md, part], md, part, gc_send, 6 + part, gp_recv, to_core)
        for slot in range(4):
            for part in (0, 1):
                arrived(slot, part, gp_recv, 1 - c)
        for keep in keeps:
            keep.wait()

    m0 = words_ref[0] | 1
    m2 = words_ref[2] | 1
    m3 = words_ref[3] | 1
    spots = lax.broadcasted_iota(jnp.int32, (2 * tile, 1), 0)
    jump = jnp.where(spots < tile, ((1 - x) * 2 + c) * block, (x * 2 + c) * block - tile)
    offsets = (spots + jump) * m0
    across = lax.broadcasted_iota(jnp.int32, (1, depth), 1) * (m0 * features)
    steps = amount // depth

    def make_signs(t, core, step):
        first = ((x * 2 + core) * amount + step * depth) * features
        base = (first + m * piece + t * tile) * m0 + words_ref[1]
        mixed = offsets + (across + base)
        mixed = (mixed ^ shifted(mixed, 15)) * m2
        mixed = (mixed ^ shifted(mixed, 13)) * m3
        return jnp.where(mixed < 0, -1.0, 1.0).astype(jnp.bfloat16)

    def columns(step):
        return pl.ds(pl.multiple_of(step * depth, depth), depth)

    def add_in(s, core, step):
        g = g2[core, :, :, :, columns(step)].reshape(group_rows, depth)
        acc[...] += lax.dot_general(
            s, g, (((1,), (1,)), ((), ())), preferred_element_type=jnp.float32
        )

    def prepare(t):
        @pl.loop(0, 2 * steps)
        def _(k):
            signs[t, k] = make_signs(t, k // steps, k % steps)

    prepare(0)
    if early > 1:
        prepare(1)
    first_halves()
    if early > 2:
        prepare(2)
    if early > 3:
        prepare(3)
    second_halves()
    last_halves()

    def slot(t, s):
        return feats.at[t, s % 4, s // 4]

    def send(t, s, sems, target):
        return rider(slot(t, s), slot(t, s), sems.at[t, s], f_recv.at[t, s], target)

    def x_copy(t):
        return rider(psend.at[t], precv.at[t], px_send.at[t], px_recv.at[t], to_x)

    def finish(t):
        x_copy(t).wait_recv()
        done = (pown[t] + precv[t]) * scale
        feats[t, m, h] = done.T.astype(jnp.bfloat16)
        pl.when(z < last)(lambda: send(t, e, up_sem, to_up).start())
        pl.when(z > 0)(lambda: send(t, e, down_sem, to_down).start())
        send(t, e, side_sem, to_y).start()

    def relay(t, hop):
        @pl.when(z >= hop)
        def _():
            low = e - 2 * hop
            send(t, low, up_sem, to_up).wait_recv()
            pl.when(z < last)(lambda: send(t, low, up_sem, to_up).start())
            send(t, low, side_sem, to_y).start()

        @pl.when(z + hop <= last)
        def _():
            high = e + 2 * hop
            send(t, high, down_sem, to_down).wait_recv()
            pl.when(z > 0)(lambda: send(t, high, down_sem, to_down).start())
            send(t, high, side_sem, to_y).start()

    def produced(t):
        psend[t] = acc[:tile]
        pown[t] = acc[tile:]
        x_copy(t).start()

    def service(t):
        pl.when(t >= 1)(lambda: finish(t - 1))
        for hop in range(1, lines):
            pl.when(t >= hop + 1)(lambda: relay(t - hop - 1, hop))

    @pl.loop(0, early)
    def _(t):
        acc[...] = jnp.zeros_like(acc)

        @pl.loop(0, 2 * steps)
        def _(k):
            add_in(signs[t, k], k // steps, k % steps)

        produced(t)
        service(t)

    @pl.loop(early, count)
    def _(t):
        acc[...] = jnp.zeros_like(acc)

        @pl.loop(0, 2 * steps)
        def _(k):
            add_in(make_signs(t, k // steps, k % steps), k // steps, k % steps)

        produced(t)
        service(t)

    for load in loads:
        load.wait()
    per = width // tile
    holder = e // (ex_n // 4)
    keeper = p == holder
    across_x = (x != holder // 2) & (c == holder % 2)
    behind = (x != holder // 2) & (c != holder % 2)

    def deal(t):
        return feats.at[t, pl.ds((e % 2) * 2, 2)]

    def deal_keep(t):
        return pltpu.make_async_copy(deal(t), mine.at[t], fe_keep.at[t])

    def deal_out(t, k):
        return rider(deal(t), mine.at[t], fe_send.at[t, k], fe_recv.at[t], (to_core, to_x)[k])

    def deal_on(t):
        return rider(mine.at[t], mine.at[t], fe_send.at[t, 0], fe_recv.at[t], to_core)

    def hand_on(t):
        @pl.when(across_x)
        def _():
            deal_on(t).wait_recv()
            deal_on(t).start()

    def multiply(t):
        for line in range(lines):
            send(t, 2 * line + 1 - y, side_sem, to_y).wait_recv()

        @pl.when(keeper)
        def _():
            deal_keep(t).start()
            deal_out(t, 1).start()
            deal_out(t, 0).start()

        if t >= 2:
            hand_on(t - 2)
        lhs = jnp.concatenate([feats[t, k].reshape(everyone, tile) for k in range(4)], axis=1)
        for q in range(4):
            cols = pl.ds(q * width, width)
            rhs = jnp.concatenate(
                [gram[k * piece + t * tile:k * piece + (t + 1) * tile, q * width:(q + 1) * width] for k in range(4)], axis=0
            )
            part = jnp.dot(lhs, rhs, preferred_element_type=jnp.float32)
            if t == 0:
                total[q] = part
            else:
                total[q] += part

    finish(count - 1)
    ready = 0
    for t in range(count, count + lines - 1):
        for hop in range(1, lines):
            if t - hop - 1 < count:
                relay(t - hop - 1, hop)
            if hop % 2 == 1 and ready < count - 2:
                multiply(ready)
                ready += 1
    relay(count - 1, last) if lines > 1 else None
    for t in range(ready, count):
        multiply(t)

    for t in range(count - 2, count):
        hand_on(t)
    rows_of = everyone // 4
    here = pl.ds(pl.multiple_of(p * rows_of, rows_of), rows_of)

    def rows(qx, qc):
        return pl.ds(pl.multiple_of((qx * 2 + qc) * rows_of, rows_of), rows_of)

    def near_copy(qx, q):
        return rider(
            total.at[q, rows(qx, 1 - c)], near.at[qx, q],
            cc_send.at[qx, q], cc_recv.at[qx, q], to_core,
        )

    def far_copy(q):
        return rider(staged.at[q], far.at[q], cx_send.at[q], cx_recv.at[q], to_x)

    def mark_copy(q):
        return rider(marks.at[q], far_marks.at[q], cm_send.at[q], cm_recv.at[q], to_x)

    for qx in (1 - x, x):
        for q in range(4):
            near_copy(qx, q).start()
    for q in range(4):
        near_copy(1 - x, q).wait_recv()
        part = total[q, rows(1 - x, c), :] + near[1 - x, q]
        most = jnp.max(jnp.abs(part), axis=1, keepdims=True)
        level = jnp.where(most > 0, 32767.0 / most, 0.0)
        staged[q] = jnp.round(part * level).astype(jnp.int32).astype(jnp.int16)
        marks[q] = jnp.broadcast_to(most * (1.0 / 32767.0), (rows_of, rows_of)).T[:8]
        mark_copy(q).start()
        far_copy(q).start()

    def got_mine(t):
        pl.when(keeper)(lambda: deal_keep(t).wait())
        pl.when(jnp.logical_not(keeper | across_x))(lambda: deal_on(t).wait_recv())

    for q in range(4):
        near_copy(x, q).wait_recv()
        part = total[q, here, :] + near[x, q]
        first = (q % 2) * per
        for t in range(first, first + per):
            if q < 2:
                got_mine(t)
        lhs = jnp.concatenate(
            [mine[t, q // 2].reshape(everyone, tile) for t in range(first, first + per)], axis=1
        )
        mark_copy(q).wait_recv()
        mark = jnp.broadcast_to(far_marks[q][:1], (rows_of, rows_of)).T
        far_copy(q).wait_recv()
        other = far[q].astype(jnp.int32).astype(jnp.float32)
        done = (part + other * jnp.concatenate([mark] * (width // rows_of), axis=1)).astype(jnp.bfloat16)
        scores = lax.dot_general(
            lhs, done, (((1,), (1,)), ((), ())), preferred_element_type=jnp.float32
        ).reshape(pairs.shape)
        if q == 0:
            pairs[...] = scores
        else:
            pairs[...] += scores

    def last_copy(k):
        peer = lax.rem(e + k, ex_n)
        return rider(pairs.at[peer], landed.at[k], s_send.at[k], s_recv.at[k], {"ex": peer})

    for k in range(1, ex_n):
        last_copy(k).start()
    final = pairs[e]
    for k in range(1, ex_n):
        last_copy(k).wait_recv()
        final += landed[k]
    out_ref[...] = final * scale

    for copy in gsends:
        copy.wait_send()
    for t in range(count):
        x_copy(t).wait_send()

        @pl.when(keeper)
        def _():
            deal_out(t, 1).wait_send()
            deal_out(t, 0).wait_send()

        pl.when(across_x)(lambda: deal_on(t).wait_send())
        send(t, e, side_sem, to_y).wait_send()
        for line in range(lines):
            s = 2 * line + y
            pl.when(line != z)(lambda: send(t, s, side_sem, to_y).wait_send())
            pl.when((z < last) & (z >= line))(lambda: send(t, s, up_sem, to_up).wait_send())
            pl.when((z > 0) & (z <= line))(lambda: send(t, s, down_sem, to_down).wait_send())
    for q in range(4):
        near_copy(0, q).wait_send()
        near_copy(1, q).wait_send()
        far_copy(q).wait_send()
        mark_copy(q).wait_send()
    for k in range(1, ex_n):
        last_copy(k).wait_send()


def fused(ex_n, par_n, gradients, inverse_gram, hash_words):
    rows, amount = gradients.shape
    block, width_e = inverse_gram.shape
    features, everyone = block * par_n, rows * ex_n
    tile, depth = 128, min(2048, amount)
    count, width, groups = block // 4 // tile, width_e // 4, ex_n // 4
    early = 4
    group = 4 * rows
    owned = everyone // 4
    vmem, dma, f32, bf16 = pltpu.VMEM, pltpu.SemaphoreType.DMA, jnp.float32, jnp.bfloat16
    return pl.pallas_call(
        functools.partial(whole_kernel, ex_n, features, tile, early, depth),
        in_specs=[
            pl.BlockSpec(memory_space=pltpu.SMEM),
            pl.BlockSpec(memory_space=pl.ANY),
            pl.BlockSpec(memory_space=pl.ANY),
        ],
        out_specs=pl.BlockSpec(memory_space=pltpu.VMEM),
        out_shape=jax.ShapeDtypeStruct((rows, owned), f32),
        scratch_shapes=[
            vmem((2, 4, 2, rows // 2, amount), bf16),
            vmem((early, 2 * amount // depth, 2 * tile, depth), bf16),
            vmem((2 * tile, group), f32),
            vmem((count, tile, group), f32),
            vmem((count, tile, group), f32),
            vmem((count, tile, group), f32),
            vmem((count, 4, groups, group, tile), bf16),
            vmem((block, width_e), bf16),
            vmem((4, everyone, width), f32),
            vmem((2, 4, owned, width), f32),
            vmem((4, owned, width), jnp.int16),
            vmem((4, owned, width), jnp.int16),
            vmem((4, 8, owned), f32),
            vmem((4, 8, owned), f32),
            vmem((count, 2, groups, group, tile), bf16),
            vmem((ex_n, rows, owned), f32),
            vmem((ex_n, rows, owned), f32),
            dma((4,)), dma((2,)), dma((3,)), dma((3,)), dma((8,)), dma((4, 2)), dma((4, 2)),
            dma((count,)), dma((count,)),
            dma((count, ex_n)), dma((count, ex_n)), dma((count, ex_n)), dma((count, ex_n)),
            dma((count, 2)), dma((count,)), dma((count,)),
            dma((2, 4)), dma((2, 4)), dma((4,)), dma((4,)), dma((4,)), dma((4,)),
            dma((ex_n,)), dma((ex_n,)),
        ],
        compiler_params=pltpu.CompilerParams(
            collective_id=7, has_side_effects=True, vmem_limit_bytes=66_000_000
        ),
    )(hash_words, gradients, inverse_gram)


def fits(ex_n, par_n, gradients, inverse_gram):
    rows = gradients.shape[0]
    block, width_e = inverse_gram.shape
    return (
        par_n == 4 and ex_n == 2 * par_n and block % 4096 == 0 and width_e % (rows * ex_n) == 0
        and rows % 32 == 0 and rows * ex_n % 512 == 0
    )


def per_device(ex_n, par_n, gradients, inverse_gram, hash_words):
    if fits(ex_n, par_n, gradients, inverse_gram):
        return fused(ex_n, par_n, gradients, inverse_gram, hash_words).T
    amount = gradients.shape[1]
    feat_par, feat_ex = inverse_gram.shape
    piece = feat_par // ex_n
    e, p = lax.axis_index("ex"), lax.axis_index("par")
    ids = jnp.arange(feat_ex, dtype=jnp.int32)
    cols = (ids // piece) * feat_par + e * piece + ids % piece
    everyone = gather(ex_n, gradients, 1).reshape(-1, amount)
    partial = project(hash_words, (p * amount)[None], cols[None, :], everyone, piece)
    mine = fold(FEATURES ** (-0.5), partial, jnp.bfloat16, 4)
    blocks = gather(ex_n, mine, 2)
    mine, blocks = lax.optimization_barrier((mine, blocks))
    pairs = []
    for src_e in range(ex_n):
        for src_p in range(par_n):
            pairs.append((src_e * par_n + src_p, src_p * ex_n + src_e))
    moved = lax.ppermute(mine, ("ex", "par"), pairs)
    parts = precondition(blocks, inverse_gram, piece)
    conditioned = fold(1.0, parts, jnp.bfloat16, 5)
    pairs = lax.dot_general(
        conditioned,
        moved,
        (((1,), (1,)), ((), ())),
        preferred_element_type=jnp.float32,
    )
    rows = fold(1.0, pairs.reshape(par_n, -1, pairs.shape[1]), jnp.float32, 6)
    return scatter(ex_n, FEATURES ** (-0.5), rows.T, 3).T


def solution(mesh):
    return jax.shard_map(
        functools.partial(per_device, mesh.shape["ex"], mesh.shape["par"]),
        mesh=mesh,
        in_specs=(P("ex", "par"), P("par", "ex"), P()),
        out_specs=P("par", "ex"),
        check_vma=False,
    )
```

```python
import functools

import jax
import jax.numpy as jnp
from jax import lax
from jax.experimental import pallas as pl
from jax.experimental.pallas import tpu as pltpu
from jax.sharding import PartitionSpec as P

FEATURES = 16384


def shifted(values, amount):
    return lax.shift_right_logical(values, jnp.full(values.shape, amount, jnp.int32))


def hash_kernel(tile, words_ref, start_ref, cols_ref, grads_ref, out_ref):
    step = pl.program_id(0)
    depth = grads_ref.shape[1]
    m0 = words_ref[0] | 1
    m2 = words_ref[2] | 1
    m3 = words_ref[3] | 1
    row_base = (start_ref[0] + step * depth) * FEATURES * m0 + words_ref[1]
    rows = lax.broadcasted_iota(jnp.int32, (depth, tile), 0) * (m0 * FEATURES)
    grads = grads_ref[...]
    for spot in range(out_ref.shape[0]):
        first = spot * tile
        mixed = rows + (cols_ref[:, first:first + tile] * m0 + row_base)
        mixed = (mixed ^ shifted(mixed, 15)) * m2
        mixed = (mixed ^ shifted(mixed, 13)) * m3
        signs = jnp.where(mixed < 0, -1.0, 1.0).astype(jnp.bfloat16)
        part = jnp.dot(grads, signs, preferred_element_type=jnp.float32)

        @pl.when(step == 0)
        def _():
            out_ref[spot] = part

        @pl.when(step > 0)
        def _():
            out_ref[spot] += part


def project(words, start, cols, grads, tile):
    rows, amount = grads.shape
    width = cols.shape[1]
    depth = min(512, amount)
    return pl.pallas_call(
        functools.partial(hash_kernel, tile),
        grid=(amount // depth,),
        in_specs=[
            pl.BlockSpec(memory_space=pltpu.SMEM),
            pl.BlockSpec(memory_space=pltpu.SMEM),
            pl.BlockSpec((1, width), lambda k: (0, 0)),
            pl.BlockSpec((rows, depth), lambda k: (0, k)),
        ],
        out_specs=pl.BlockSpec((width // tile, rows, tile), lambda k: (0, 0, 0)),
        out_shape=jax.ShapeDtypeStruct((width // tile, rows, tile), jnp.float32),
        compiler_params=pltpu.CompilerParams(
            dimension_semantics=("arbitrary",), vmem_limit_bytes=48 << 20
        ),
    )(words, start, cols, grads)


MESH = pl.DeviceIdType.MESH


def gather_kernel(ex_n, own_ref, out_ref, keep_sem, up_sem, down_sem, side_sem, recv_sem):
    e = lax.axis_index("ex")
    line, side = e // 2, e % 2
    last = ex_n // 2 - 1
    above, below, beside = lax.rem(e + 2, ex_n), lax.rem(e + ex_n - 2, ex_n), line * 2 + 1 - side
    barrier = pltpu.get_barrier_semaphore()

    def greet(peer):
        pl.semaphore_signal(barrier, inc=1, device_id={"ex": peer}, device_id_type=MESH)

    greet(beside)
    pl.when(line < last)(lambda: greet(above))
    pl.when(line > 0)(lambda: greet(below))
    inside = (line > 0) & (line < last)
    pl.when(inside)(lambda: pl.semaphore_wait(barrier, 3))
    pl.when(jnp.logical_not(inside))(lambda: pl.semaphore_wait(barrier, 2))

    def copy(src, slot, sems, peer):
        return pltpu.make_async_remote_copy(
            src_ref=src,
            dst_ref=out_ref.at[slot],
            send_sem=sems.at[slot],
            recv_sem=recv_sem.at[slot],
            device_id={"ex": peer},
            device_id_type=MESH,
        )

    keep = pltpu.make_async_copy(own_ref, out_ref.at[e], keep_sem)
    keep.start()
    pl.when(line < last)(lambda: copy(own_ref, e, up_sem, above).start())
    pl.when(line > 0)(lambda: copy(own_ref, e, down_sem, below).start())
    copy(own_ref, e, side_sem, beside).start()
    for far in range(1, last + 1):
        low, high = e - 2 * far, e + 2 * far

        @pl.when(line >= far)
        def _():
            copy(out_ref.at[low], low, up_sem, above).wait_recv()
            pl.when(line < last)(lambda: copy(out_ref.at[low], low, up_sem, above).start())
            copy(out_ref.at[low], low, side_sem, beside).start()

        @pl.when(line + far <= last)
        def _():
            copy(out_ref.at[high], high, down_sem, below).wait_recv()
            pl.when(line > 0)(lambda: copy(out_ref.at[high], high, down_sem, below).start())
            copy(out_ref.at[high], high, side_sem, beside).start()

    for spot in range(last + 1):
        mine, other = 2 * spot + side, 2 * spot + 1 - side
        copy(out_ref.at[other], other, side_sem, beside).wait_recv()
        copy(out_ref.at[mine], mine, side_sem, beside).wait_send()

        @pl.when((line < last) & (line >= spot))
        def _():
            copy(out_ref.at[mine], mine, up_sem, above).wait_send()

        @pl.when((line > 0) & (line <= spot))
        def _():
            copy(out_ref.at[mine], mine, down_sem, below).wait_send()

    keep.wait()


def gather(ex_n, own, collective_id):
    return pl.pallas_call(
        functools.partial(gather_kernel, ex_n),
        in_specs=[pl.BlockSpec(memory_space=pltpu.VMEM)],
        out_specs=pl.BlockSpec(memory_space=pl.ANY),
        out_shape=jax.ShapeDtypeStruct((ex_n,) + own.shape, own.dtype),
        scratch_shapes=[pltpu.SemaphoreType.DMA]
        + [pltpu.SemaphoreType.DMA((ex_n,)) for _ in range(4)],
        compiler_params=pltpu.CompilerParams(
            collective_id=collective_id, has_side_effects=True, vmem_limit_bytes=8 << 20
        ),
    )(own)


def scatter_kernel(ex_n, scale, in_ref, out_ref, landed, send_sem, recv_sem):
    e = lax.axis_index("ex")
    rows = out_ref.shape[0]
    barrier = pltpu.get_barrier_semaphore()
    for far in range(1, ex_n):
        peer = lax.rem(e + far, ex_n)
        pl.semaphore_signal(barrier, inc=1, device_id={"ex": peer}, device_id_type=MESH)
    pl.semaphore_wait(barrier, ex_n - 1)
    copies = []
    for far in range(1, ex_n):
        peer = lax.rem(e + far, ex_n)
        copies.append(
            pltpu.make_async_remote_copy(
                src_ref=in_ref.at[pl.ds(pl.multiple_of(peer * rows, rows), rows)],
                dst_ref=landed.at[far],
                send_sem=send_sem.at[far],
                recv_sem=recv_sem.at[far],
                device_id={"ex": peer},
                device_id_type=MESH,
            )
        )
        copies[-1].start()
    total = in_ref[pl.ds(pl.multiple_of(e * rows, rows), rows), :]
    for far in range(1, ex_n):
        copies[far - 1].wait_recv()
        total += landed[far]
    out_ref[...] = total * scale
    for each in copies:
        each.wait_send()


def scatter(ex_n, scale, stacked, collective_id):
    rows, columns = stacked.shape[0] // ex_n, stacked.shape[1]
    return pl.pallas_call(
        functools.partial(scatter_kernel, ex_n, scale),
        in_specs=[pl.BlockSpec(memory_space=pltpu.VMEM)],
        out_specs=pl.BlockSpec(memory_space=pltpu.VMEM),
        out_shape=jax.ShapeDtypeStruct((rows, columns), jnp.float32),
        scratch_shapes=[
            pltpu.VMEM((ex_n, rows, columns), jnp.float32),
            pltpu.SemaphoreType.DMA((ex_n,)),
            pltpu.SemaphoreType.DMA((ex_n,)),
        ],
        compiler_params=pltpu.CompilerParams(
            collective_id=collective_id, has_side_effects=True, vmem_limit_bytes=16 << 20
        ),
    )(stacked)


def fold_kernel(chips, cuts, scale, in_ref, out_ref, near, staged, landed, near_send, near_recv, far_send, far_recv):
    p = lax.axis_index("par")
    x, core = p // 2, p % 2
    rows = in_ref.shape[1] // cuts
    partner = x * 2 + 1 - core
    barrier = pltpu.get_barrier_semaphore()
    pl.semaphore_signal(barrier, inc=1, device_id={"par": partner}, device_id_type=MESH)
    for d in range(1, chips):
        peer = lax.rem(x + d, chips) * 2 + core
        pl.semaphore_signal(barrier, inc=1, device_id={"par": peer}, device_id_type=MESH)
    pl.semaphore_wait(barrier, chips)
    order = [(d, c) for d in list(range(1, chips)) + [0] for c in range(cuts)]
    across, onward = {}, {}
    for d, c in order:
        part = pl.ds(c * rows, rows)
        across[d, c] = pltpu.make_async_remote_copy(
            src_ref=in_ref.at[lax.rem(x + d, chips) * 2 + 1 - core, part],
            dst_ref=near.at[d, part],
            send_sem=near_send.at[d, c],
            recv_sem=near_recv.at[d, c],
            device_id={"par": partner},
            device_id_type=MESH,
        )
        across[d, c].start()
    for d, c in order:
        part = pl.ds(c * rows, rows)
        across[d, c].wait_recv()
        total = in_ref[lax.rem(x + d, chips) * 2 + core, part, :] + near[d, part, :]
        staged[d, part, :] = total
        if d > 0:
            onward[d, c] = pltpu.make_async_remote_copy(
                src_ref=staged.at[d, part],
                dst_ref=landed.at[d, part],
                send_sem=far_send.at[d, c],
                recv_sem=far_recv.at[d, c],
                device_id={"par": lax.rem(x + d, chips) * 2 + core},
                device_id_type=MESH,
            )
            onward[d, c].start()
    for c in range(cuts):
        part = pl.ds(c * rows, rows)
        total = staged[0, part, :]
        for d in range(1, chips):
            onward[d, c].wait_recv()
            total += landed[d, part, :]
        out_ref[part, :] = (total * scale).astype(out_ref.dtype)
    for each in list(across.values()) + list(onward.values()):
        each.wait_send()


def fold(scale, stacked, dtype, collective_id):
    par_n, rows, columns = stacked.shape
    chips = par_n // 2
    cuts = 8 if rows * columns >= 1 << 18 else 2
    hold = pltpu.VMEM((chips, rows, columns), jnp.float32)
    return pl.pallas_call(
        functools.partial(fold_kernel, chips, cuts, scale),
        in_specs=[pl.BlockSpec(memory_space=pltpu.VMEM)],
        out_specs=pl.BlockSpec(memory_space=pltpu.VMEM),
        out_shape=jax.ShapeDtypeStruct((rows, columns), dtype),
        scratch_shapes=[hold, hold, hold]
        + [pltpu.SemaphoreType.DMA((chips, cuts)) for _ in range(4)],
        compiler_params=pltpu.CompilerParams(
            collective_id=collective_id, has_side_effects=True, vmem_limit_bytes=48 << 20
        ),
    )(stacked)


def tiles_kernel(feat_ref, gram_ref, out_ref):
    step = pl.program_id(0)
    tile = out_ref.shape[2]
    for spot in range(out_ref.shape[0]):
        gram = gram_ref[:, spot * tile:(spot + 1) * tile]
        part = jnp.dot(feat_ref[0], gram, preferred_element_type=jnp.float32)

        @pl.when(step == 0)
        def _():
            out_ref[spot] = part

        @pl.when(step > 0)
        def _():
            out_ref[spot] += part


def precondition(blocks, gram, tile):
    count, rows, piece = blocks.shape
    width = gram.shape[1]
    return pl.pallas_call(
        tiles_kernel,
        grid=(count,),
        in_specs=[
            pl.BlockSpec((1, rows, piece), lambda k: (k, 0, 0)),
            pl.BlockSpec((piece, width), lambda k: (k, 0)),
        ],
        out_specs=pl.BlockSpec((width // tile, rows, tile), lambda k: (0, 0, 0)),
        out_shape=jax.ShapeDtypeStruct((width // tile, rows, tile), jnp.float32),
        compiler_params=pltpu.CompilerParams(
            dimension_semantics=("arbitrary",), vmem_limit_bytes=48 << 20
        ),
        cost_estimate=pl.CostEstimate(
            flops=2 * count * rows * piece * width,
            bytes_accessed=2 * count * piece * (rows + width) + 4 * rows * width,
            transcendentals=0,
        ),
    )(blocks, gram)


def rider(src, dst, send_sem, recv_sem, device_id):
    return pltpu.make_async_remote_copy(
        src_ref=src, dst_ref=dst, send_sem=send_sem, recv_sem=recv_sem,
        device_id=device_id, device_id_type=MESH,
    )


def whole_kernel(
    ex_n, features, tile, early, depth, words_ref, grads_ref, gram_ref, out_ref,
    g2, signs, acc, psend, pown, precv, feats, gram, total, near, staged, far, marks, far_marks,
    mine, pairs, landed,
    gram_sem, keep_sem, gy_send, gz_send, gc_send, g_recv, gp_recv, px_send, px_recv,
    up_sem, down_sem, side_sem, f_recv, fe_send, fe_recv, fe_keep,
    cc_send, cc_recv, cx_send, cx_recv, cm_send, cm_recv, s_send, s_recv,
):
    e, p = lax.axis_index("ex"), lax.axis_index("par")
    z, y, x, c, h, m = e // 2, e % 2, p // 2, p % 2, e // 4, e % 4
    lines, groups = ex_n // 2, ex_n // 4
    last = lines - 1
    half = g2.shape[3]
    amount = g2.shape[4]
    count = feats.shape[0]
    group_rows = feats.shape[3]
    block = gram.shape[0]
    piece = block // 4
    everyone, width = total.shape[1], total.shape[2]
    scale = features ** -0.5

    def others(own, n):
        return [lax.rem(own + d, n) for d in range(1, n)]

    barrier = pltpu.get_barrier_semaphore()
    for peer in others(e, ex_n):
        pl.semaphore_signal(barrier, inc=1, device_id={"ex": peer}, device_id_type=MESH)
    for peer in others(p, 4):
        pl.semaphore_signal(barrier, inc=1, device_id={"par": peer}, device_id_type=MESH)
    pl.semaphore_wait(barrier, ex_n + 2)

    to_y, to_z = {"ex": e + 1 - 2 * y}, {"ex": e + 2 - 4 * (z % 2)}
    to_core, to_x = {"par": x * 2 + 1 - c}, {"par": (1 - x) * 2 + c}
    to_up, to_down = {"ex": lax.rem(e + 2, ex_n)}, {"ex": lax.rem(e + ex_n - 2, ex_n)}
    my, mz, md = m + 1 - 2 * (m % 2), m + 2 - 4 * (m // 2), 3 - m

    gsends = []

    def gcopy(src, slot, part, sems, k, recv, target):
        copy = rider(src, g2.at[c, slot, part], sems.at[k], recv.at[slot, part], target)
        copy.start()
        gsends.append(copy)

    own = [grads_ref.at[pl.ds(part * half, half)] for part in (0, 1)]
    keeps = [pltpu.make_async_copy(own[part], g2.at[c, m, part], keep_sem.at[part]) for part in (0, 1)]
    gcopy(own[0], m, 0, gy_send, 0, g_recv, to_y)
    gcopy(own[1], m, 1, gz_send, 0, g_recv, to_z)
    gcopy(own[1], m, 1, gy_send, 1, g_recv, to_y)
    gcopy(own[0], m, 0, gz_send, 1, g_recv, to_z)
    for part in (0, 1):
        keeps[part].start()
        gcopy(own[part], m, part, gc_send, part, gp_recv, to_core)
    loads = []
    for k in range(4):
        rows = pl.ds(k * piece, piece)
        loads.append(pltpu.make_async_copy(gram_ref.at[rows], gram.at[rows], gram_sem.at[k]))
        loads[-1].start()

    def arrived(slot, part, recv, core):
        spot = g2.at[core, slot, part]
        rider(spot, spot, gy_send.at[0], recv.at[slot, part], to_y).wait_recv()

    def first_halves():
        arrived(my, 0, g_recv, c)
        gcopy(g2.at[c, my, 0], my, 0, gz_send, 2, g_recv, to_z)
        gcopy(g2.at[c, my, 0], my, 0, gc_send, 2, gp_recv, to_core)
        arrived(mz, 1, g_recv, c)
        gcopy(g2.at[c, mz, 1], mz, 1, gy_send, 2, g_recv, to_y)
        gcopy(g2.at[c, mz, 1], mz, 1, gc_send, 3, gp_recv, to_core)

    def second_halves():
        arrived(my, 1, g_recv, c)
        gcopy(g2.at[c, my, 1], my, 1, gc_send, 4, gp_recv, to_core)
        arrived(mz, 0, g_recv, c)
        gcopy(g2.at[c, mz, 0], mz, 0, gc_send, 5, gp_recv, to_core)

    def last_halves():
        for part in (0, 1):
            arrived(md, part, g_recv, c)
            gcopy(g2.at[c, md, part], md, part, gc_send, 6 + part, gp_recv, to_core)
        for slot in range(4):
            for part in (0, 1):
                arrived(slot, part, gp_recv, 1 - c)
        for keep in keeps:
            keep.wait()

    m0 = words_ref[0] | 1
    m2 = words_ref[2] | 1
    m3 = words_ref[3] | 1
    spots = lax.broadcasted_iota(jnp.int32, (2 * tile, 1), 0)
    jump = jnp.where(spots < tile, ((1 - x) * 2 + c) * block, (x * 2 + c) * block - tile)
    offsets = (spots + jump) * m0
    across = lax.broadcasted_iota(jnp.int32, (1, depth), 1) * (m0 * features)
    steps = amount // depth

    def make_signs(t, core, step):
        first = ((x * 2 + core) * amount + step * depth) * features
        base = (first + m * piece + t * tile) * m0 + words_ref[1]
        mixed = offsets + (across + base)
        mixed = (mixed ^ shifted(mixed, 15)) * m2
        mixed = (mixed ^ shifted(mixed, 13)) * m3
        return jnp.where(mixed < 0, -1.0, 1.0).astype(jnp.bfloat16)

    def columns(step):
        return pl.ds(pl.multiple_of(step * depth, depth), depth)

    def add_in(s, core, step):
        g = g2[core, :, :, :, columns(step)].reshape(group_rows, depth)
        acc[...] += lax.dot_general(
            s, g, (((1,), (1,)), ((), ())), preferred_element_type=jnp.float32
        )

    def prepare(t):
        @pl.loop(0, 2 * steps)
        def _(k):
            signs[t, k] = make_signs(t, k // steps, k % steps)

    prepare(0)
    if early > 1:
        prepare(1)
    first_halves()
    if early > 2:
        prepare(2)
    if early > 3:
        prepare(3)
    second_halves()
    last_halves()

    def slot(t, s):
        return feats.at[t, s % 4, s // 4]

    def send(t, s, sems, target):
        return rider(slot(t, s), slot(t, s), sems.at[t, s], f_recv.at[t, s], target)

    def x_copy(t):
        return rider(psend.at[t], precv.at[t], px_send.at[t], px_recv.at[t], to_x)

    def finish(t):
        x_copy(t).wait_recv()
        done = (pown[t] + precv[t]) * scale
        feats[t, m, h] = done.T.astype(jnp.bfloat16)
        pl.when(z < last)(lambda: send(t, e, up_sem, to_up).start())
        pl.when(z > 0)(lambda: send(t, e, down_sem, to_down).start())
        send(t, e, side_sem, to_y).start()

    def bends(t):
        return (t % 2 == 1) & (t < count - 1)

    def crosses(t, line):
        return jnp.logical_not(bends(t)) | ((line > 0) & (line < last))

    def relay(t, hop):
        @pl.when(z >= hop)
        def _():
            low = e - 2 * hop
            send(t, low, up_sem, to_up).wait_recv()
            pl.when(z < last)(lambda: send(t, low, up_sem, to_up).start())
            pl.when(crosses(t, z - hop))(lambda: send(t, low, side_sem, to_y).start())

        @pl.when(z + hop <= last)
        def _():
            high = e + 2 * hop
            send(t, high, down_sem, to_down).wait_recv()
            pl.when(z > 0)(lambda: send(t, high, down_sem, to_down).start())
            pl.when(crosses(t, z + hop))(lambda: send(t, high, side_sem, to_y).start())

    first_far, last_far = 1 - y, 2 * last + 1 - y

    def detour(t, hop):
        @pl.when(bends(t) & (t > 0) & (z == hop - 1))
        def _():
            send(t, first_far, up_sem, to_up).wait_recv()
            pl.when(z < last)(lambda: send(t, first_far, up_sem, to_up).start())

        @pl.when(bends(t) & (t > 0) & (last - z == hop - 1))
        def _():
            send(t, last_far, down_sem, to_down).wait_recv()
            pl.when(z > 0)(lambda: send(t, last_far, down_sem, to_down).start())

    def produced(t):
        psend[t] = acc[:tile]
        pown[t] = acc[tile:]
        x_copy(t).start()

    def service(t):
        pl.when(t >= 1)(lambda: finish(t - 1))
        for hop in range(1, lines):
            pl.when(t >= hop + 1)(lambda: relay(t - hop - 1, hop))
        for hop in range(1, lines):
            detour(t - hop - 2, hop)

    @pl.loop(0, early)
    def _(t):
        acc[...] = jnp.zeros_like(acc)

        @pl.loop(0, 2 * steps)
        def _(k):
            add_in(signs[t, k], k // steps, k % steps)

        produced(t)
        service(t)

    @pl.loop(early, count)
    def _(t):
        acc[...] = jnp.zeros_like(acc)

        @pl.loop(0, 2 * steps)
        def _(k):
            add_in(make_signs(t, k // steps, k % steps), k // steps, k % steps)

        produced(t)
        service(t)

    for load in loads:
        load.wait()
    per = width // tile
    holder = e // (ex_n // 4)
    keeper = p == holder
    across_x = (x != holder // 2) & (c == holder % 2)
    behind = (x != holder // 2) & (c != holder % 2)

    def deal(t):
        return feats.at[t, pl.ds((e % 2) * 2, 2)]

    def deal_keep(t):
        return pltpu.make_async_copy(deal(t), mine.at[t], fe_keep.at[t])

    def deal_out(t, k):
        return rider(deal(t), mine.at[t], fe_send.at[t, k], fe_recv.at[t], (to_core, to_x)[k])

    def deal_on(t):
        return rider(mine.at[t], mine.at[t], fe_send.at[t, 0], fe_recv.at[t], to_core)

    def hand_on(t):
        @pl.when(across_x)
        def _():
            deal_on(t).wait_recv()
            deal_on(t).start()

    def multiply(t):
        bent = t % 2 == 1 and t < count - 1
        if bent:
            detour(t, lines)
        for line in range(lines):
            if not bent or 0 < line < last:
                send(t, 2 * line + 1 - y, side_sem, to_y).wait_recv()

        @pl.when(keeper)
        def _():
            deal_keep(t).start()
            deal_out(t, 0).start()
            if t < count - 1:
                deal_out(t, 1).start()

        if t >= 2:
            hand_on(t - 2)
        lhs = jnp.concatenate([feats[t, k].reshape(everyone, tile) for k in range(4)], axis=1)
        for q in range(4):
            cols = pl.ds(q * width, width)
            rhs = jnp.concatenate(
                [gram[k * piece + t * tile:k * piece + (t + 1) * tile, q * width:(q + 1) * width] for k in range(4)], axis=0
            )
            part = jnp.dot(lhs, rhs, preferred_element_type=jnp.float32)
            if t == 0:
                total[q] = part
            else:
                total[q] += part

    finish(count - 1)
    ready = 0
    for t in range(count, count + lines):
        for hop in range(1, lines):
            if t - hop - 1 < count:
                relay(t - hop - 1, hop)
            if (t - hop - 2) % 2 == 1 and t - hop - 2 < count - 1:
                detour(t - hop - 2, hop)
            if hop % 2 == 1 and ready < count - 4:
                multiply(ready)
                ready += 1
    for t in range(ready, count):
        multiply(t)

    rows_of = everyone // 4
    here = pl.ds(pl.multiple_of(p * rows_of, rows_of), rows_of)

    def rows(qx, qc):
        return pl.ds(pl.multiple_of((qx * 2 + qc) * rows_of, rows_of), rows_of)

    def near_copy(qx, q):
        return rider(
            total.at[q, rows(qx, 1 - c)], near.at[qx, q],
            cc_send.at[qx, q], cc_recv.at[qx, q], to_core,
        )

    def far_copy(q):
        return rider(staged.at[q], far.at[q], cx_send.at[q], cx_recv.at[q], to_x)

    def mark_copy(q):
        return rider(marks.at[q], far_marks.at[q], cm_send.at[q], cm_recv.at[q], to_x)

    sequence = (0, 2, 1, 3)
    for qx in (1 - x, x):
        for q in sequence:
            near_copy(qx, q).start()
    for q in sequence:
        near_copy(1 - x, q).wait_recv()
        part = total[q, rows(1 - x, c), :] + near[1 - x, q]
        most = jnp.max(jnp.abs(part), axis=1, keepdims=True)
        level = jnp.where(most > 0, 32767.0 / most, 0.0)
        staged[q] = jnp.round(part * level).astype(jnp.int32).astype(jnp.int16)
        marks[q] = jnp.broadcast_to(most * (1.0 / 32767.0), (rows_of, rows_of)).T[:8]
        mark_copy(q).start()
        far_copy(q).start()
        if q == sequence[2]:
            pl.when(keeper)(lambda: deal_out(count - 1, 1).start())
    for t in range(count - 2, count):
        hand_on(t)

    def got_mine(t):
        pl.when(keeper)(lambda: deal_keep(t).wait())
        pl.when(jnp.logical_not(keeper | across_x))(lambda: deal_on(t).wait_recv())

    for q in sequence:
        near_copy(x, q).wait_recv()
        part = total[q, here, :] + near[x, q]
        first = (q % 2) * per
        for t in range(first, first + per):
            if q < 2:
                got_mine(t)
        lhs = jnp.concatenate(
            [mine[t, q // 2].reshape(everyone, tile) for t in range(first, first + per)], axis=1
        )
        mark_copy(q).wait_recv()
        mark = jnp.broadcast_to(far_marks[q][:1], (rows_of, rows_of)).T
        far_copy(q).wait_recv()
        other = far[q].astype(jnp.int32).astype(jnp.float32)
        done = (part + other * jnp.concatenate([mark] * (width // rows_of), axis=1)).astype(jnp.bfloat16)
        scores = lax.dot_general(
            lhs, done, (((1,), (1,)), ((), ())), preferred_element_type=jnp.float32
        ).reshape(pairs.shape)
        if q == 0:
            pairs[...] = scores
        else:
            pairs[...] += scores

    def last_copy(k):
        peer = lax.rem(e + k, ex_n)
        return rider(pairs.at[peer], landed.at[k], s_send.at[k], s_recv.at[k], {"ex": peer})

    for k in range(1, ex_n):
        last_copy(k).start()
    final = pairs[e]
    for k in range(1, ex_n):
        last_copy(k).wait_recv()
        final += landed[k]
    out_ref[...] = final * scale

    for copy in gsends:
        copy.wait_send()
    for t in range(count):
        x_copy(t).wait_send()

        @pl.when(keeper)
        def _():
            deal_out(t, 1).wait_send()
            deal_out(t, 0).wait_send()

        pl.when(across_x)(lambda: deal_on(t).wait_send())
        send(t, e, side_sem, to_y).wait_send()
        bent = t % 2 == 1 and t < count - 1
        if bent:
            pl.when(z < last)(lambda: send(t, first_far, up_sem, to_up).wait_send())
            pl.when(z > 0)(lambda: send(t, last_far, down_sem, to_down).wait_send())
        for line in range(lines):
            s = 2 * line + y
            if not bent or 0 < line < last:
                pl.when(line != z)(lambda: send(t, s, side_sem, to_y).wait_send())
            pl.when((z < last) & (z >= line))(lambda: send(t, s, up_sem, to_up).wait_send())
            pl.when((z > 0) & (z <= line))(lambda: send(t, s, down_sem, to_down).wait_send())
    for q in range(4):
        near_copy(0, q).wait_send()
        near_copy(1, q).wait_send()
        far_copy(q).wait_send()
        mark_copy(q).wait_send()
    for k in range(1, ex_n):
        last_copy(k).wait_send()


def fused(ex_n, par_n, gradients, inverse_gram, hash_words):
    rows, amount = gradients.shape
    block, width_e = inverse_gram.shape
    features, everyone = block * par_n, rows * ex_n
    tile, depth = 128, min(2048, amount)
    count, width, groups = block // 4 // tile, width_e // 4, ex_n // 4
    early = 4
    group = 4 * rows
    owned = everyone // 4
    vmem, dma, f32, bf16 = pltpu.VMEM, pltpu.SemaphoreType.DMA, jnp.float32, jnp.bfloat16
    return pl.pallas_call(
        functools.partial(whole_kernel, ex_n, features, tile, early, depth),
        in_specs=[
            pl.BlockSpec(memory_space=pltpu.SMEM),
            pl.BlockSpec(memory_space=pl.ANY),
            pl.BlockSpec(memory_space=pl.ANY),
        ],
        out_specs=pl.BlockSpec(memory_space=pltpu.VMEM),
        out_shape=jax.ShapeDtypeStruct((rows, owned), f32),
        scratch_shapes=[
            vmem((2, 4, 2, rows // 2, amount), bf16),
            vmem((early, 2 * amount // depth, 2 * tile, depth), bf16),
            vmem((2 * tile, group), f32),
            vmem((count, tile, group), f32),
            vmem((count, tile, group), f32),
            vmem((count, tile, group), f32),
            vmem((count, 4, groups, group, tile), bf16),
            vmem((block, width_e), bf16),
            vmem((4, everyone, width), f32),
            vmem((2, 4, owned, width), f32),
            vmem((4, owned, width), jnp.int16),
            vmem((4, owned, width), jnp.int16),
            vmem((4, 8, owned), f32),
            vmem((4, 8, owned), f32),
            vmem((count, 2, groups, group, tile), bf16),
            vmem((ex_n, rows, owned), f32),
            vmem((ex_n, rows, owned), f32),
            dma((4,)), dma((2,)), dma((3,)), dma((3,)), dma((8,)), dma((4, 2)), dma((4, 2)),
            dma((count,)), dma((count,)),
            dma((count, ex_n)), dma((count, ex_n)), dma((count, ex_n)), dma((count, ex_n)),
            dma((count, 2)), dma((count,)), dma((count,)),
            dma((2, 4)), dma((2, 4)), dma((4,)), dma((4,)), dma((4,)), dma((4,)),
            dma((ex_n,)), dma((ex_n,)),
        ],
        compiler_params=pltpu.CompilerParams(
            collective_id=7, has_side_effects=True, vmem_limit_bytes=66_000_000
        ),
    )(hash_words, gradients, inverse_gram)


def fits(ex_n, par_n, gradients, inverse_gram):
    rows = gradients.shape[0]
    block, width_e = inverse_gram.shape
    return (
        par_n == 4 and ex_n == 2 * par_n and block % 4096 == 0 and width_e % (rows * ex_n) == 0
        and rows % 32 == 0 and rows * ex_n % 512 == 0
    )


def per_device(ex_n, par_n, gradients, inverse_gram, hash_words):
    if fits(ex_n, par_n, gradients, inverse_gram):
        return fused(ex_n, par_n, gradients, inverse_gram, hash_words).T
    amount = gradients.shape[1]
    feat_par, feat_ex = inverse_gram.shape
    piece = feat_par // ex_n
    e, p = lax.axis_index("ex"), lax.axis_index("par")
    ids = jnp.arange(feat_ex, dtype=jnp.int32)
    cols = (ids // piece) * feat_par + e * piece + ids % piece
    everyone = gather(ex_n, gradients, 1).reshape(-1, amount)
    partial = project(hash_words, (p * amount)[None], cols[None, :], everyone, piece)
    mine = fold(FEATURES ** (-0.5), partial, jnp.bfloat16, 4)
    blocks = gather(ex_n, mine, 2)
    mine, blocks = lax.optimization_barrier((mine, blocks))
    pairs = []
    for src_e in range(ex_n):
        for src_p in range(par_n):
            pairs.append((src_e * par_n + src_p, src_p * ex_n + src_e))
    moved = lax.ppermute(mine, ("ex", "par"), pairs)
    parts = precondition(blocks, inverse_gram, piece)
    conditioned = fold(1.0, parts, jnp.bfloat16, 5)
    pairs = lax.dot_general(
        conditioned,
        moved,
        (((1,), (1,)), ((), ())),
        preferred_element_type=jnp.float32,
    )
    rows = fold(1.0, pairs.reshape(par_n, -1, pairs.shape[1]), jnp.float32, 6)
    return scatter(ex_n, FEATURES ** (-0.5), rows.T, 3).T


def solution(mesh):
    return jax.shard_map(
        functools.partial(per_device, mesh.shape["ex"], mesh.shape["par"]),
        mesh=mesh,
        in_specs=(P("ex", "par"), P("par", "ex"), P()),
        out_specs=P("par", "ex"),
        check_vma=False,
    )
```

```python
import functools

import jax
import jax.numpy as jnp
from jax import lax
from jax.experimental import pallas as pl
from jax.experimental.pallas import tpu as pltpu
from jax.sharding import PartitionSpec as P

FEATURES = 16384


def shifted(values, amount):
    return lax.shift_right_logical(values, jnp.full(values.shape, amount, jnp.int32))


def hash_kernel(tile, words_ref, start_ref, cols_ref, grads_ref, out_ref):
    step = pl.program_id(0)
    depth = grads_ref.shape[1]
    m0 = words_ref[0] | 1
    m2 = words_ref[2] | 1
    m3 = words_ref[3] | 1
    row_base = (start_ref[0] + step * depth) * FEATURES * m0 + words_ref[1]
    rows = lax.broadcasted_iota(jnp.int32, (depth, tile), 0) * (m0 * FEATURES)
    grads = grads_ref[...]
    for spot in range(out_ref.shape[0]):
        first = spot * tile
        mixed = rows + (cols_ref[:, first:first + tile] * m0 + row_base)
        mixed = (mixed ^ shifted(mixed, 15)) * m2
        mixed = (mixed ^ shifted(mixed, 13)) * m3
        signs = jnp.where(mixed < 0, -1.0, 1.0).astype(jnp.bfloat16)
        part = jnp.dot(grads, signs, preferred_element_type=jnp.float32)

        @pl.when(step == 0)
        def _():
            out_ref[spot] = part

        @pl.when(step > 0)
        def _():
            out_ref[spot] += part


def project(words, start, cols, grads, tile):
    rows, amount = grads.shape
    width = cols.shape[1]
    depth = min(512, amount)
    return pl.pallas_call(
        functools.partial(hash_kernel, tile),
        grid=(amount // depth,),
        in_specs=[
            pl.BlockSpec(memory_space=pltpu.SMEM),
            pl.BlockSpec(memory_space=pltpu.SMEM),
            pl.BlockSpec((1, width), lambda k: (0, 0)),
            pl.BlockSpec((rows, depth), lambda k: (0, k)),
        ],
        out_specs=pl.BlockSpec((width // tile, rows, tile), lambda k: (0, 0, 0)),
        out_shape=jax.ShapeDtypeStruct((width // tile, rows, tile), jnp.float32),
        compiler_params=pltpu.CompilerParams(
            dimension_semantics=("arbitrary",), vmem_limit_bytes=48 << 20
        ),
    )(words, start, cols, grads)


MESH = pl.DeviceIdType.MESH


def gather_kernel(ex_n, own_ref, out_ref, keep_sem, up_sem, down_sem, side_sem, recv_sem):
    e = lax.axis_index("ex")
    line, side = e // 2, e % 2
    last = ex_n // 2 - 1
    above, below, beside = lax.rem(e + 2, ex_n), lax.rem(e + ex_n - 2, ex_n), line * 2 + 1 - side
    barrier = pltpu.get_barrier_semaphore()

    def greet(peer):
        pl.semaphore_signal(barrier, inc=1, device_id={"ex": peer}, device_id_type=MESH)

    greet(beside)
    pl.when(line < last)(lambda: greet(above))
    pl.when(line > 0)(lambda: greet(below))
    inside = (line > 0) & (line < last)
    pl.when(inside)(lambda: pl.semaphore_wait(barrier, 3))
    pl.when(jnp.logical_not(inside))(lambda: pl.semaphore_wait(barrier, 2))

    def copy(src, slot, sems, peer):
        return pltpu.make_async_remote_copy(
            src_ref=src,
            dst_ref=out_ref.at[slot],
            send_sem=sems.at[slot],
            recv_sem=recv_sem.at[slot],
            device_id={"ex": peer},
            device_id_type=MESH,
        )

    keep = pltpu.make_async_copy(own_ref, out_ref.at[e], keep_sem)
    keep.start()
    pl.when(line < last)(lambda: copy(own_ref, e, up_sem, above).start())
    pl.when(line > 0)(lambda: copy(own_ref, e, down_sem, below).start())
    copy(own_ref, e, side_sem, beside).start()
    for far in range(1, last + 1):
        low, high = e - 2 * far, e + 2 * far

        @pl.when(line >= far)
        def _():
            copy(out_ref.at[low], low, up_sem, above).wait_recv()
            pl.when(line < last)(lambda: copy(out_ref.at[low], low, up_sem, above).start())
            copy(out_ref.at[low], low, side_sem, beside).start()

        @pl.when(line + far <= last)
        def _():
            copy(out_ref.at[high], high, down_sem, below).wait_recv()
            pl.when(line > 0)(lambda: copy(out_ref.at[high], high, down_sem, below).start())
            copy(out_ref.at[high], high, side_sem, beside).start()

    for spot in range(last + 1):
        mine, other = 2 * spot + side, 2 * spot + 1 - side
        copy(out_ref.at[other], other, side_sem, beside).wait_recv()
        copy(out_ref.at[mine], mine, side_sem, beside).wait_send()

        @pl.when((line < last) & (line >= spot))
        def _():
            copy(out_ref.at[mine], mine, up_sem, above).wait_send()

        @pl.when((line > 0) & (line <= spot))
        def _():
            copy(out_ref.at[mine], mine, down_sem, below).wait_send()

    keep.wait()


def gather(ex_n, own, collective_id):
    return pl.pallas_call(
        functools.partial(gather_kernel, ex_n),
        in_specs=[pl.BlockSpec(memory_space=pltpu.VMEM)],
        out_specs=pl.BlockSpec(memory_space=pl.ANY),
        out_shape=jax.ShapeDtypeStruct((ex_n,) + own.shape, own.dtype),
        scratch_shapes=[pltpu.SemaphoreType.DMA]
        + [pltpu.SemaphoreType.DMA((ex_n,)) for _ in range(4)],
        compiler_params=pltpu.CompilerParams(
            collective_id=collective_id, has_side_effects=True, vmem_limit_bytes=8 << 20
        ),
    )(own)


def scatter_kernel(ex_n, scale, in_ref, out_ref, landed, send_sem, recv_sem):
    e = lax.axis_index("ex")
    rows = out_ref.shape[0]
    barrier = pltpu.get_barrier_semaphore()
    for far in range(1, ex_n):
        peer = lax.rem(e + far, ex_n)
        pl.semaphore_signal(barrier, inc=1, device_id={"ex": peer}, device_id_type=MESH)
    pl.semaphore_wait(barrier, ex_n - 1)
    copies = []
    for far in range(1, ex_n):
        peer = lax.rem(e + far, ex_n)
        copies.append(
            pltpu.make_async_remote_copy(
                src_ref=in_ref.at[pl.ds(pl.multiple_of(peer * rows, rows), rows)],
                dst_ref=landed.at[far],
                send_sem=send_sem.at[far],
                recv_sem=recv_sem.at[far],
                device_id={"ex": peer},
                device_id_type=MESH,
            )
        )
        copies[-1].start()
    total = in_ref[pl.ds(pl.multiple_of(e * rows, rows), rows), :]
    for far in range(1, ex_n):
        copies[far - 1].wait_recv()
        total += landed[far]
    out_ref[...] = total * scale
    for each in copies:
        each.wait_send()


def scatter(ex_n, scale, stacked, collective_id):
    rows, columns = stacked.shape[0] // ex_n, stacked.shape[1]
    return pl.pallas_call(
        functools.partial(scatter_kernel, ex_n, scale),
        in_specs=[pl.BlockSpec(memory_space=pltpu.VMEM)],
        out_specs=pl.BlockSpec(memory_space=pltpu.VMEM),
        out_shape=jax.ShapeDtypeStruct((rows, columns), jnp.float32),
        scratch_shapes=[
            pltpu.VMEM((ex_n, rows, columns), jnp.float32),
            pltpu.SemaphoreType.DMA((ex_n,)),
            pltpu.SemaphoreType.DMA((ex_n,)),
        ],
        compiler_params=pltpu.CompilerParams(
            collective_id=collective_id, has_side_effects=True, vmem_limit_bytes=16 << 20
        ),
    )(stacked)


def fold_kernel(chips, cuts, scale, in_ref, out_ref, near, staged, landed, near_send, near_recv, far_send, far_recv):
    p = lax.axis_index("par")
    x, core = p // 2, p % 2
    rows = in_ref.shape[1] // cuts
    partner = x * 2 + 1 - core
    barrier = pltpu.get_barrier_semaphore()
    pl.semaphore_signal(barrier, inc=1, device_id={"par": partner}, device_id_type=MESH)
    for d in range(1, chips):
        peer = lax.rem(x + d, chips) * 2 + core
        pl.semaphore_signal(barrier, inc=1, device_id={"par": peer}, device_id_type=MESH)
    pl.semaphore_wait(barrier, chips)
    order = [(d, c) for d in list(range(1, chips)) + [0] for c in range(cuts)]
    across, onward = {}, {}
    for d, c in order:
        part = pl.ds(c * rows, rows)
        across[d, c] = pltpu.make_async_remote_copy(
            src_ref=in_ref.at[lax.rem(x + d, chips) * 2 + 1 - core, part],
            dst_ref=near.at[d, part],
            send_sem=near_send.at[d, c],
            recv_sem=near_recv.at[d, c],
            device_id={"par": partner},
            device_id_type=MESH,
        )
        across[d, c].start()
    for d, c in order:
        part = pl.ds(c * rows, rows)
        across[d, c].wait_recv()
        total = in_ref[lax.rem(x + d, chips) * 2 + core, part, :] + near[d, part, :]
        staged[d, part, :] = total
        if d > 0:
            onward[d, c] = pltpu.make_async_remote_copy(
                src_ref=staged.at[d, part],
                dst_ref=landed.at[d, part],
                send_sem=far_send.at[d, c],
                recv_sem=far_recv.at[d, c],
                device_id={"par": lax.rem(x + d, chips) * 2 + core},
                device_id_type=MESH,
            )
            onward[d, c].start()
    for c in range(cuts):
        part = pl.ds(c * rows, rows)
        total = staged[0, part, :]
        for d in range(1, chips):
            onward[d, c].wait_recv()
            total += landed[d, part, :]
        out_ref[part, :] = (total * scale).astype(out_ref.dtype)
    for each in list(across.values()) + list(onward.values()):
        each.wait_send()


def fold(scale, stacked, dtype, collective_id):
    par_n, rows, columns = stacked.shape
    chips = par_n // 2
    cuts = 8 if rows * columns >= 1 << 18 else 2
    hold = pltpu.VMEM((chips, rows, columns), jnp.float32)
    return pl.pallas_call(
        functools.partial(fold_kernel, chips, cuts, scale),
        in_specs=[pl.BlockSpec(memory_space=pltpu.VMEM)],
        out_specs=pl.BlockSpec(memory_space=pltpu.VMEM),
        out_shape=jax.ShapeDtypeStruct((rows, columns), dtype),
        scratch_shapes=[hold, hold, hold]
        + [pltpu.SemaphoreType.DMA((chips, cuts)) for _ in range(4)],
        compiler_params=pltpu.CompilerParams(
            collective_id=collective_id, has_side_effects=True, vmem_limit_bytes=48 << 20
        ),
    )(stacked)


def tiles_kernel(feat_ref, gram_ref, out_ref):
    step = pl.program_id(0)
    tile = out_ref.shape[2]
    for spot in range(out_ref.shape[0]):
        gram = gram_ref[:, spot * tile:(spot + 1) * tile]
        part = jnp.dot(feat_ref[0], gram, preferred_element_type=jnp.float32)

        @pl.when(step == 0)
        def _():
            out_ref[spot] = part

        @pl.when(step > 0)
        def _():
            out_ref[spot] += part


def precondition(blocks, gram, tile):
    count, rows, piece = blocks.shape
    width = gram.shape[1]
    return pl.pallas_call(
        tiles_kernel,
        grid=(count,),
        in_specs=[
            pl.BlockSpec((1, rows, piece), lambda k: (k, 0, 0)),
            pl.BlockSpec((piece, width), lambda k: (k, 0)),
        ],
        out_specs=pl.BlockSpec((width // tile, rows, tile), lambda k: (0, 0, 0)),
        out_shape=jax.ShapeDtypeStruct((width // tile, rows, tile), jnp.float32),
        compiler_params=pltpu.CompilerParams(
            dimension_semantics=("arbitrary",), vmem_limit_bytes=48 << 20
        ),
        cost_estimate=pl.CostEstimate(
            flops=2 * count * rows * piece * width,
            bytes_accessed=2 * count * piece * (rows + width) + 4 * rows * width,
            transcendentals=0,
        ),
    )(blocks, gram)


def rider(src, dst, send_sem, recv_sem, device_id):
    return pltpu.make_async_remote_copy(
        src_ref=src, dst_ref=dst, send_sem=send_sem, recv_sem=recv_sem,
        device_id=device_id, device_id_type=MESH,
    )


def whole_kernel(
    ex_n, features, tile, early, depth, words_ref, grads_ref, gram_ref, out_ref,
    g2, signs, acc, psend, pown, precv, feats, gram, total, near, staged, far, marks, far_marks,
    mine, pairs, landed,
    gram_sem, keep_sem, gy_send, gz_send, gc_send, g_recv, gp_recv, px_send, px_recv,
    up_sem, down_sem, side_sem, f_recv, fe_send, fe_recv, fe_keep,
    cc_send, cc_recv, cx_send, cx_recv, cm_send, cm_recv, s_send, s_recv,
):
    e, p = lax.axis_index("ex"), lax.axis_index("par")
    z, y, x, c, h, m = e // 2, e % 2, p // 2, p % 2, e // 4, e % 4
    lines, groups = ex_n // 2, ex_n // 4
    last = lines - 1
    half = g2.shape[3]
    amount = g2.shape[4]
    count = feats.shape[0]
    group_rows = feats.shape[3]
    block = gram.shape[0]
    piece = block // 4
    everyone, width = total.shape[1], total.shape[2]
    scale = features ** -0.5

    def others(own, n):
        return [lax.rem(own + d, n) for d in range(1, n)]

    barrier = pltpu.get_barrier_semaphore()
    for peer in others(e, ex_n):
        pl.semaphore_signal(barrier, inc=1, device_id={"ex": peer}, device_id_type=MESH)
    for peer in others(p, 4):
        pl.semaphore_signal(barrier, inc=1, device_id={"par": peer}, device_id_type=MESH)
    e_far = lax.rem(e + 4, ex_n)
    to_far = {"ex": e_far, "par": lax.rem(p + 2, 4)}
    pl.semaphore_signal(barrier, inc=1, device_id=to_far, device_id_type=MESH)
    pl.semaphore_wait(barrier, ex_n + 3)

    to_y, to_z = {"ex": e + 1 - 2 * y}, {"ex": e + 2 - 4 * (z % 2)}
    to_core, to_x = {"par": x * 2 + 1 - c}, {"par": (1 - x) * 2 + c}
    to_up, to_down = {"ex": lax.rem(e + 2, ex_n)}, {"ex": lax.rem(e + ex_n - 2, ex_n)}
    my, mz, md = m + 1 - 2 * (m % 2), m + 2 - 4 * (m // 2), 3 - m

    gsends = []

    def gcopy(src, slot, part, sems, k, recv, target):
        copy = rider(src, g2.at[c, slot, part], sems.at[k], recv.at[slot, part], target)
        copy.start()
        gsends.append(copy)

    own = [grads_ref.at[pl.ds(part * half, half)] for part in (0, 1)]
    keeps = [pltpu.make_async_copy(own[part], g2.at[c, m, part], keep_sem.at[part]) for part in (0, 1)]
    gcopy(own[0], m, 0, gy_send, 0, g_recv, to_y)
    gcopy(own[1], m, 1, gz_send, 0, g_recv, to_z)
    gcopy(own[1], m, 1, gy_send, 1, g_recv, to_y)
    gcopy(own[0], m, 0, gz_send, 1, g_recv, to_z)
    for part in (0, 1):
        keeps[part].start()
        gcopy(own[part], m, part, gc_send, part, gp_recv, to_core)
    loads = []
    for k in range(4):
        rows = pl.ds(k * piece, piece)
        loads.append(pltpu.make_async_copy(gram_ref.at[rows], gram.at[rows], gram_sem.at[k]))
        loads[-1].start()

    def arrived(slot, part, recv, core):
        spot = g2.at[core, slot, part]
        rider(spot, spot, gy_send.at[0], recv.at[slot, part], to_y).wait_recv()

    def first_halves():
        arrived(my, 0, g_recv, c)
        gcopy(g2.at[c, my, 0], my, 0, gz_send, 2, g_recv, to_z)
        gcopy(g2.at[c, my, 0], my, 0, gc_send, 2, gp_recv, to_core)
        arrived(mz, 1, g_recv, c)
        gcopy(g2.at[c, mz, 1], mz, 1, gy_send, 2, g_recv, to_y)
        gcopy(g2.at[c, mz, 1], mz, 1, gc_send, 3, gp_recv, to_core)

    def second_halves():
        arrived(my, 1, g_recv, c)
        gcopy(g2.at[c, my, 1], my, 1, gc_send, 4, gp_recv, to_core)
        arrived(mz, 0, g_recv, c)
        gcopy(g2.at[c, mz, 0], mz, 0, gc_send, 5, gp_recv, to_core)

    def last_halves():
        for part in (0, 1):
            arrived(md, part, g_recv, c)
            gcopy(g2.at[c, md, part], md, part, gc_send, 6 + part, gp_recv, to_core)
        for keep in keeps:
            keep.wait()

    def partner_halves():
        for slot in range(4):
            for part in (0, 1):
                arrived(slot, part, gp_recv, 1 - c)

    m0 = words_ref[0] | 1
    m2 = words_ref[2] | 1
    m3 = words_ref[3] | 1
    spots = lax.broadcasted_iota(jnp.int32, (2 * tile, 1), 0)
    jump = jnp.where(spots < tile, ((1 - x) * 2 + c) * block, (x * 2 + c) * block - tile)
    offsets = (spots + jump) * m0
    across = lax.broadcasted_iota(jnp.int32, (1, depth), 1) * (m0 * features)
    steps = amount // depth

    def make_signs(t, core, step):
        first = ((x * 2 + core) * amount + step * depth) * features
        base = (first + m * piece + t * tile) * m0 + words_ref[1]
        mixed = offsets + (across + base)
        mixed = (mixed ^ shifted(mixed, 15)) * m2
        mixed = (mixed ^ shifted(mixed, 13)) * m3
        return jnp.where(mixed < 0, -1.0, 1.0).astype(jnp.bfloat16)

    def columns(step):
        return pl.ds(pl.multiple_of(step * depth, depth), depth)

    def add_in(s, core, step):
        g = g2[core, :, :, :, columns(step)].reshape(group_rows, depth)
        acc[...] += lax.dot_general(
            s, g, (((1,), (1,)), ((), ())), preferred_element_type=jnp.float32
        )

    def prepare(t):
        @pl.loop(0, 2 * steps)
        def _(k):
            signs[t, k] = make_signs(t, k // steps, k % steps)

    prepare(0)
    if early > 1:
        prepare(1)
    first_halves()
    if early > 2:
        prepare(2)
    if early > 3:
        prepare(3)
    second_halves()
    last_halves()

    def slot(t, s):
        return feats.at[t, s % 4, s // 4]

    def send(t, s, sems, target):
        return rider(slot(t, s), slot(t, s), sems.at[t, s], f_recv.at[t, s], target)

    def x_copy(t):
        return rider(psend.at[t], precv.at[t], px_send.at[t], px_recv.at[t], to_x)

    def finish(t):
        x_copy(t).wait_recv()
        done = (pown[t] + precv[t]) * scale
        feats[t, m, h] = done.T.astype(jnp.bfloat16)
        pl.when(z < last)(lambda: send(t, e, up_sem, to_up).start())
        pl.when(z > 0)(lambda: send(t, e, down_sem, to_down).start())
        send(t, e, side_sem, to_y).start()

    def bends(t):
        return (t % 2 == 1) & (t < count - 1)

    def crosses(t, line):
        return jnp.logical_not(bends(t)) | ((line > 0) & (line < last))

    def relay(t, hop):
        @pl.when(z >= hop)
        def _():
            low = e - 2 * hop
            send(t, low, up_sem, to_up).wait_recv()
            pl.when(z < last)(lambda: send(t, low, up_sem, to_up).start())
            pl.when(crosses(t, z - hop))(lambda: send(t, low, side_sem, to_y).start())

        @pl.when(z + hop <= last)
        def _():
            high = e + 2 * hop
            send(t, high, down_sem, to_down).wait_recv()
            pl.when(z > 0)(lambda: send(t, high, down_sem, to_down).start())
            pl.when(crosses(t, z + hop))(lambda: send(t, high, side_sem, to_y).start())

    first_far, last_far = 1 - y, 2 * last + 1 - y

    def detour(t, hop):
        @pl.when(bends(t) & (t > 0) & (z == hop - 1))
        def _():
            send(t, first_far, up_sem, to_up).wait_recv()
            pl.when(z < last)(lambda: send(t, first_far, up_sem, to_up).start())

        @pl.when(bends(t) & (t > 0) & (last - z == hop - 1))
        def _():
            send(t, last_far, down_sem, to_down).wait_recv()
            pl.when(z > 0)(lambda: send(t, last_far, down_sem, to_down).start())

    def produced(t):
        psend[t] = acc[:tile]
        pown[t] = acc[tile:]
        x_copy(t).start()

    def service(t):
        pl.when(t >= 1)(lambda: finish(t - 1))
        for hop in range(1, lines):
            pl.when(t >= hop + 1)(lambda: relay(t - hop - 1, hop))
        for hop in range(1, lines):
            detour(t - hop - 2, hop)

    acc[...] = jnp.zeros_like(acc)
    for turn in (0, 1):
        core = c if turn == 0 else 1 - c

        @pl.loop(0, steps)
        def _(k):
            add_in(signs[0, core * steps + k], core, k)

        if turn == 0:
            partner_halves()
    produced(0)

    @pl.loop(1, early)
    def _(t):
        acc[...] = jnp.zeros_like(acc)

        @pl.loop(0, 2 * steps)
        def _(k):
            add_in(signs[t, k], k // steps, k % steps)

        produced(t)
        service(t)

    @pl.loop(early, count)
    def _(t):
        acc[...] = jnp.zeros_like(acc)

        @pl.loop(0, 2 * steps)
        def _(k):
            add_in(make_signs(t, k // steps, k % steps), k // steps, k % steps)

        produced(t)
        service(t)

    for load in loads:
        load.wait()
    per = width // tile
    holder = e // (ex_n // 4)
    keeper = p == holder
    across_x = (x != holder // 2) & (c == holder % 2)
    behind = (x != holder // 2) & (c != holder % 2)

    def deal(t):
        return feats.at[t, pl.ds((e % 2) * 2, 2)]

    def deal_keep(t):
        return pltpu.make_async_copy(deal(t), mine.at[t], fe_keep.at[t])

    def deal_out(t, k):
        return rider(deal(t), mine.at[t], fe_send.at[t, k], fe_recv.at[t], (to_core, to_x)[k])

    far_keeper = p == e_far // (ex_n // 4)

    def far_deal(t):
        return rider(deal(t), mine.at[t], fe_send.at[t, 1], fe_recv.at[t], to_far)

    def goes_far(t):
        return t >= count // 2 and t % 2 == 1

    def deal_over(t, act):
        if goes_far(t):
            pl.when(far_keeper)(lambda: act(far_deal(t)))
        else:
            pl.when(keeper)(lambda: act(deal_out(t, 1)))

    def deal_on(t):
        return rider(mine.at[t], mine.at[t], fe_send.at[t, 0], fe_recv.at[t], to_core)

    def hand_on(t):
        @pl.when(across_x)
        def _():
            deal_on(t).wait_recv()
            deal_on(t).start()

    rows_of = everyone // 4
    here = pl.ds(pl.multiple_of(p * rows_of, rows_of), rows_of)

    def rows(qx, qc):
        return pl.ds(pl.multiple_of((qx * 2 + qc) * rows_of, rows_of), rows_of)

    def near_copy(qx, q):
        return rider(
            total.at[q, rows(qx, 1 - c)], near.at[qx, q],
            cc_send.at[qx, q], cc_recv.at[qx, q], to_core,
        )

    def far_copy(q):
        return rider(staged.at[q], far.at[q], cx_send.at[q], cx_recv.at[q], to_x)

    def mark_copy(q):
        return rider(marks.at[q], far_marks.at[q], cm_send.at[q], cm_recv.at[q], to_x)

    sequence = (0, 2, 1, 3)
    def multiply(t):
        bent = t % 2 == 1 and t < count - 1
        if bent:
            detour(t, lines)
        for line in range(lines):
            if not bent or 0 < line < last:
                send(t, 2 * line + 1 - y, side_sem, to_y).wait_recv()

        @pl.when(keeper)
        def _():
            deal_keep(t).start()
            deal_out(t, 0).start()

        if t < count - 1:
            deal_over(t, lambda copy: copy.start())

        if t >= 4:
            hand_on(t - 4)
        lhs = jnp.concatenate([feats[t, k].reshape(everyone, tile) for k in range(4)], axis=1)
        for q in sequence:
            rhs = jnp.concatenate(
                [gram[k * piece + t * tile:k * piece + (t + 1) * tile, q * width:(q + 1) * width] for k in range(4)], axis=0
            )
            part = jnp.dot(lhs, rhs, preferred_element_type=jnp.float32)
            if t == 0:
                total[q] = part
            else:
                total[q] += part
            if t == count - 1:
                near_copy(1 - x, q).start()

    finish(count - 1)
    ready = 0
    for t in range(count, count + lines):
        for hop in range(1, lines):
            if t - hop - 1 < count:
                relay(t - hop - 1, hop)
            if (t - hop - 2) % 2 == 1 and t - hop - 2 < count - 1:
                detour(t - hop - 2, hop)
            if hop % 2 == 1 and ready < count - 4:
                multiply(ready)
                ready += 1
    for t in range(ready, count):
        multiply(t)

    for q in sequence:
        near_copy(x, q).start()
    for q in sequence:
        near_copy(1 - x, q).wait_recv()
        part = total[q, rows(1 - x, c), :] + near[1 - x, q]
        most = jnp.max(jnp.abs(part), axis=1, keepdims=True)
        level = jnp.where(most > 0, 32767.0 / most, 0.0)
        staged[q] = jnp.round(part * level).astype(jnp.int32).astype(jnp.int16)
        marks[q] = jnp.broadcast_to(most * (1.0 / 32767.0), (rows_of, rows_of)).T[:8]
        mark_copy(q).start()
        far_copy(q).start()
        if q == sequence[2]:
            deal_over(count - 1, lambda copy: copy.start())
    for t in range(count - 4, count):
        hand_on(t)

    def got_mine(t):
        pl.when(keeper)(lambda: deal_keep(t).wait())
        pl.when(jnp.logical_not(keeper | across_x))(lambda: deal_on(t).wait_recv())

    for q in sequence:
        near_copy(x, q).wait_recv()
        part = total[q, here, :] + near[x, q]
        first = (q % 2) * per
        for t in range(first, first + per):
            if q < 2:
                got_mine(t)
        lhs = jnp.concatenate(
            [mine[t, q // 2].reshape(everyone, tile) for t in range(first, first + per)], axis=1
        )
        mark_copy(q).wait_recv()
        mark = jnp.broadcast_to(far_marks[q][:1], (rows_of, rows_of)).T
        far_copy(q).wait_recv()
        other = far[q].astype(jnp.int32).astype(jnp.float32)
        done = (part + other * jnp.concatenate([mark] * (width // rows_of), axis=1)).astype(jnp.bfloat16)
        scores = lax.dot_general(
            lhs, done, (((1,), (1,)), ((), ())), preferred_element_type=jnp.float32
        ).reshape(pairs.shape)
        if q == 0:
            pairs[...] = scores
        else:
            pairs[...] += scores

    def last_copy(k):
        peer = lax.rem(e + k, ex_n)
        return rider(pairs.at[peer], landed.at[k], s_send.at[k], s_recv.at[k], {"ex": peer})

    for k in range(1, ex_n):
        last_copy(k).start()
    final = pairs[e]
    for k in range(1, ex_n):
        last_copy(k).wait_recv()
        final += landed[k]
    out_ref[...] = final * scale

    for copy in gsends:
        copy.wait_send()
    for t in range(count):
        x_copy(t).wait_send()

        deal_over(t, lambda copy: copy.wait_send())
        pl.when(keeper)(lambda: deal_out(t, 0).wait_send())

        pl.when(across_x)(lambda: deal_on(t).wait_send())
        send(t, e, side_sem, to_y).wait_send()
        bent = t % 2 == 1 and t < count - 1
        if bent:
            pl.when(z < last)(lambda: send(t, first_far, up_sem, to_up).wait_send())
            pl.when(z > 0)(lambda: send(t, last_far, down_sem, to_down).wait_send())
        for line in range(lines):
            s = 2 * line + y
            if not bent or 0 < line < last:
                pl.when(line != z)(lambda: send(t, s, side_sem, to_y).wait_send())
            pl.when((z < last) & (z >= line))(lambda: send(t, s, up_sem, to_up).wait_send())
            pl.when((z > 0) & (z <= line))(lambda: send(t, s, down_sem, to_down).wait_send())
    for q in range(4):
        near_copy(0, q).wait_send()
        near_copy(1, q).wait_send()
        far_copy(q).wait_send()
        mark_copy(q).wait_send()
    for k in range(1, ex_n):
        last_copy(k).wait_send()


def fused(ex_n, par_n, gradients, inverse_gram, hash_words):
    rows, amount = gradients.shape
    block, width_e = inverse_gram.shape
    features, everyone = block * par_n, rows * ex_n
    tile, depth = 128, min(2048, amount)
    count, width, groups = block // 4 // tile, width_e // 4, ex_n // 4
    early = 4
    group = 4 * rows
    owned = everyone // 4
    vmem, dma, f32, bf16 = pltpu.VMEM, pltpu.SemaphoreType.DMA, jnp.float32, jnp.bfloat16
    return pl.pallas_call(
        functools.partial(whole_kernel, ex_n, features, tile, early, depth),
        in_specs=[
            pl.BlockSpec(memory_space=pltpu.SMEM),
            pl.BlockSpec(memory_space=pl.ANY),
            pl.BlockSpec(memory_space=pl.ANY),
        ],
        out_specs=pl.BlockSpec(memory_space=pltpu.VMEM),
        out_shape=jax.ShapeDtypeStruct((rows, owned), f32),
        scratch_shapes=[
            vmem((2, 4, 2, rows // 2, amount), bf16),
            vmem((early, 2 * amount // depth, 2 * tile, depth), bf16),
            vmem((2 * tile, group), f32),
            vmem((count, tile, group), f32),
            vmem((count, tile, group), f32),
            vmem((count, tile, group), f32),
            vmem((count, 4, groups, group, tile), bf16),
            vmem((block, width_e), bf16),
            vmem((4, everyone, width), f32),
            vmem((2, 4, owned, width), f32),
            vmem((4, owned, width), jnp.int16),
            vmem((4, owned, width), jnp.int16),
            vmem((4, 8, owned), f32),
            vmem((4, 8, owned), f32),
            vmem((count, 2, groups, group, tile), bf16),
            vmem((ex_n, rows, owned), f32),
            vmem((ex_n, rows, owned), f32),
            dma((4,)), dma((2,)), dma((3,)), dma((3,)), dma((8,)), dma((4, 2)), dma((4, 2)),
            dma((count,)), dma((count,)),
            dma((count, ex_n)), dma((count, ex_n)), dma((count, ex_n)), dma((count, ex_n)),
            dma((count, 2)), dma((count,)), dma((count,)),
            dma((2, 4)), dma((2, 4)), dma((4,)), dma((4,)), dma((4,)), dma((4,)),
            dma((ex_n,)), dma((ex_n,)),
        ],
        compiler_params=pltpu.CompilerParams(
            collective_id=7, has_side_effects=True, vmem_limit_bytes=66_000_000
        ),
    )(hash_words, gradients, inverse_gram)


def fits(ex_n, par_n, gradients, inverse_gram):
    rows = gradients.shape[0]
    block, width_e = inverse_gram.shape
    return (
        par_n == 4 and ex_n == 2 * par_n and block % 4096 == 0 and width_e % (rows * ex_n) == 0
        and rows % 32 == 0 and rows * ex_n % 512 == 0
    )


def per_device(ex_n, par_n, gradients, inverse_gram, hash_words):
    if fits(ex_n, par_n, gradients, inverse_gram):
        return fused(ex_n, par_n, gradients, inverse_gram, hash_words).T
    amount = gradients.shape[1]
    feat_par, feat_ex = inverse_gram.shape
    piece = feat_par // ex_n
    e, p = lax.axis_index("ex"), lax.axis_index("par")
    ids = jnp.arange(feat_ex, dtype=jnp.int32)
    cols = (ids // piece) * feat_par + e * piece + ids % piece
    everyone = gather(ex_n, gradients, 1).reshape(-1, amount)
    partial = project(hash_words, (p * amount)[None], cols[None, :], everyone, piece)
    mine = fold(FEATURES ** (-0.5), partial, jnp.bfloat16, 4)
    blocks = gather(ex_n, mine, 2)
    mine, blocks = lax.optimization_barrier((mine, blocks))
    pairs = []
    for src_e in range(ex_n):
        for src_p in range(par_n):
            pairs.append((src_e * par_n + src_p, src_p * ex_n + src_e))
    moved = lax.ppermute(mine, ("ex", "par"), pairs)
    parts = precondition(blocks, inverse_gram, piece)
    conditioned = fold(1.0, parts, jnp.bfloat16, 5)
    pairs = lax.dot_general(
        conditioned,
        moved,
        (((1,), (1,)), ((), ())),
        preferred_element_type=jnp.float32,
    )
    rows = fold(1.0, pairs.reshape(par_n, -1, pairs.shape[1]), jnp.float32, 6)
    return scatter(ex_n, FEATURES ** (-0.5), rows.T, 3).T


def solution(mesh):
    return jax.shard_map(
        functools.partial(per_device, mesh.shape["ex"], mesh.shape["par"]),
        mesh=mesh,
        in_specs=(P("ex", "par"), P("par", "ex"), P()),
        out_specs=P("par", "ex"),
        check_vma=False,
    )
```
